256 devices in a mesh: ctx: 32 (over x, z), kvh: 8 (over y, core).
Axes of the slice: x: 4, y: 4, z: 8, core: 2. Of those that a mesh axis runs over, the one named last changes fastest.
Arguments:
- queries: bfloat16 [12, 16, 8192], P(None, None, 'kvh'), may hold values from -100 to 100
- keys: bfloat16 [2048, 8, 256, 128], P('ctx', 'kvh'), may hold values from -8 to 8
- values: bfloat16 [2048, 8, 256, 128], P('ctx', 'kvh'), may hold values from -6 to 6
- out_weight: bfloat16 [8192, 8192], P('kvh', 'ctx'), may hold values from -0.0625 to 0.0625
- lengths: int32 [12], replicated, may hold values from 16 to 16384, as said below
- slot_request: int32 [2048], P('ctx'), may hold values from 0 to 12, as said below
- slot_page: int32 [2048], P('ctx'), may hold values from 0 to 63, as said below
Outputs:
- projected: bfloat16 [192, 8192], P('kvh', 'ctx')
The draws below stay inside these ranges and needn't reach their ends.
Inputs may be any that keep to these rules, and one draw needn't show every extreme that they name: `lengths`: some request has length 16 and some request has length 16384. slot_request is 12 for an empty slot; each page 0 to (lengths[r] - 1) // 256 of request r stands in exactly one slot, and no other page of it does. `slot_page`: 0 for an empty slot.
All inputs are finite; a program needn't handle non-finite values.
Results may differ from the reference program's by a relative error of at most 0.015.
Values may be sent and summed in bfloat16 or wider, within the bound.
A program may use at most 128 MiB of HBM per device.

```python
import math
import jax
import jax.numpy as jnp
from jax import lax

D = 8192
QUERY_HEADS = 64
KEY_VALUE_HEADS = 8
HEAD_SIZE = 128
REQUEST_COUNT = 12
DRAFT_TOKENS = 16
PAGE_TOKENS = 256
PAGES_DEV = 64
PAGE_SLOTS = 2048
N_CTX = 32


def layout(key):
    base = jax.random.fold_in(key, 7001)
    parts = jax.random.split(base, 6)
    slot_ids = jnp.arange(PAGE_SLOTS, dtype=jnp.int32)
    device_ids = jnp.arange(N_CTX, dtype=jnp.int32)
    fullest = jax.random.randint(parts[0], (), 0, N_CTX)
    powers = jax.random.randint(parts[1], (N_CTX,), 0, 4)
    powers = jnp.where(device_ids == fullest, 3, powers)
    live_count = jnp.array([1, 2, 4, 8], dtype=jnp.int32)[powers] * PAGES_DEV // 8
    owner_dev = slot_ids // PAGES_DEV
    live = slot_ids % PAGES_DEV < live_count[owner_dev]
    live_total = jnp.sum(live_count)
    request_ids = jnp.arange(REQUEST_COUNT, dtype=jnp.int32)
    heaviest = jax.random.randint(parts[2], (), 0, REQUEST_COUNT)
    lightest = (heaviest + 1) % REQUEST_COUNT
    others = (request_ids != heaviest) & (request_ids != lightest)
    shares = jax.random.randint(parts[3], (REQUEST_COUNT,), 1, 25)
    shares = jnp.where(others, shares, 0)
    spare = live_total - REQUEST_COUNT - PAGES_DEV
    extra = shares * spare // jnp.maximum(jnp.sum(shares), 1)
    counts = jnp.minimum(extra + 1, PAGES_DEV)
    counts = jnp.where(request_ids == heaviest, PAGES_DEV, counts)
    counts = jnp.where(request_ids == lightest, 1, counts)
    starts = jnp.cumsum(counts) - counts
    used = jnp.sum(counts)
    priority = jnp.where(live, jax.random.permutation(parts[4], PAGE_SLOTS).astype(jnp.int32), PAGE_SLOTS + slot_ids)
    ranks = jnp.argsort(jnp.argsort(priority)).astype(jnp.int32)
    holds = ranks < used
    owner_req = jnp.sum((starts[None, :] <= ranks[:, None]).astype(jnp.int32), axis=1) - 1
    owner_safe = jnp.clip(owner_req, 0, REQUEST_COUNT - 1)
    slot_request = jnp.where(holds, owner_req, REQUEST_COUNT).astype(jnp.int32)
    slot_page = jnp.where(holds, ranks - starts[owner_safe], 0).astype(jnp.int32)
    tails = jax.random.randint(parts[5], (REQUEST_COUNT,), DRAFT_TOKENS, PAGE_TOKENS + 1)
    tails = jnp.where(request_ids == heaviest, PAGE_TOKENS, tails)
    tails = jnp.where(request_ids == lightest, DRAFT_TOKENS, tails)
    lengths = ((counts - 1) * PAGE_TOKENS + tails).astype(jnp.int32)
    return (lengths, slot_request, slot_page)


def draw_lengths(key, part):
    return layout(key)[0]


def draw_slot_request(key, part):
    return layout(key)[1]


def draw_slot_page(key, part):
    return layout(key)[2]


def draw_keys(key, part):
    random_noise_key = jax.random.fold_in(key, 9201)
    return jnp.clip(jax.random.normal(random_noise_key, (PAGE_SLOTS, KEY_VALUE_HEADS, PAGE_TOKENS, HEAD_SIZE), jnp.float32), -6.0, 6.0).astype(jnp.bfloat16)


def draw_queries(key, part):
    streams = jax.random.split(jax.random.fold_in(key, 9301), 2)
    head_scale = jnp.exp(jax.random.uniform(streams[0], (QUERY_HEADS,), jnp.float32, math.log(0.5), math.log(20.0)))
    head_scale = jnp.repeat(head_scale, HEAD_SIZE)
    normal_part = jnp.clip(jax.random.normal(streams[1], (REQUEST_COUNT, DRAFT_TOKENS, QUERY_HEADS * HEAD_SIZE), jnp.float32), -6.0, 6.0)
    return jnp.clip(normal_part * head_scale, -100.0, 100.0).astype(jnp.bfloat16)


def level_of(stream_key, shape, pieces, low, top_value):
    def one(axis_at, blocks):
        draws = jax.random.uniform(jax.random.fold_in(jax.random.fold_in(stream_key, 6), axis_at), (blocks,), jnp.float32, low / len(pieces), top_value / len(pieces))
        return jnp.repeat(jnp.exp(draws), shape[axis_at] // blocks).reshape((-1,) + (1,) * (len(shape) - axis_at - 1))

    factor_of = one(*pieces[0])
    for cut in pieces[1:]:
        factor_of = factor_of * one(*cut)
    return factor_of


def gaussian(own_key, shape, deviation, reach, shards=(), kind=jnp.bfloat16):
    result = jax.random.normal(own_key, shape, jnp.float32) * deviation
    if len(shards) > 0:
        result = level_of(own_key, shape, shards, -0.22, 0.18) * result
    return jnp.clip(result, min=-reach, max=reach).astype(kind)


def setup_inputs(seed: int = 0) -> dict:
    key_of = jax.random.split(jax.random.key(seed), 8)
    queries = draw_queries(jax.random.fold_in(key_of[7], 71), 0)
    keys = draw_keys(jax.random.fold_in(key_of[7], 71), 0)
    values = gaussian(key_of[2], (PAGE_SLOTS, KEY_VALUE_HEADS, PAGE_TOKENS, HEAD_SIZE), 1.0, 6.0, ((0, 32), (1, 8)))
    out_weight = gaussian(key_of[3], (QUERY_HEADS * HEAD_SIZE, D), (QUERY_HEADS * HEAD_SIZE) ** -0.5, 0.0625, ((0, 8), (1, 32)))
    lengths = draw_lengths(jax.random.fold_in(key_of[7], 71), 0)
    slot_request = draw_slot_request(jax.random.fold_in(key_of[7], 71), 0)
    slot_page = draw_slot_page(jax.random.fold_in(key_of[7], 71), 0)
    return {"queries": queries, "keys": keys, "values": values, "out_weight": out_weight, "lengths": lengths, "slot_request": slot_request, "slot_page": slot_page}


NEGATIVE_FLOOR = -1e+30
PRECISE = lax.Precision.HIGHEST

def reference(queries, keys, values, out_weight, lengths, slot_request, slot_page):
    query_group_width = QUERY_HEADS // KEY_VALUE_HEADS
    query_matrix_rows = DRAFT_TOKENS * query_group_width
    score_scale = 1.0 / math.sqrt(HEAD_SIZE)
    query_lookup_table = queries.reshape(REQUEST_COUNT, DRAFT_TOKENS, KEY_VALUE_HEADS, query_group_width, HEAD_SIZE).transpose(0, 2, 1, 3, 4).reshape(REQUEST_COUNT, KEY_VALUE_HEADS, query_matrix_rows, HEAD_SIZE).astype(jnp.float32)
    pages_per_block = 8
    block_total = keys.shape[0] // pages_per_block
    key_cache_blocks = keys.reshape(block_total, pages_per_block, KEY_VALUE_HEADS, PAGE_TOKENS, HEAD_SIZE)
    value_cache_blocks = values.reshape(block_total, pages_per_block, KEY_VALUE_HEADS, PAGE_TOKENS, HEAD_SIZE)
    request_blocks = slot_request.reshape(block_total, pages_per_block)
    index_blocks = slot_page.reshape(block_total, pages_per_block)
    draft_row = jnp.arange(query_matrix_rows, dtype=jnp.int32) // query_group_width
    token_index = jnp.arange(PAGE_TOKENS, dtype=jnp.int32)
    request_ids = jnp.arange(REQUEST_COUNT, dtype=jnp.int32)

    def visit(running, block_data):
        maxima, running_totals, output_rows = running
        key_block, value_block, page_request, page_index = block_data
        belongs = page_request[:, None] == request_ids[None, :]
        onehot = belongs.astype(jnp.float32)
        chosen = jnp.einsum('br,rhqd->bhqd', onehot, query_lookup_table, precision=PRECISE)
        scores = jnp.einsum('bhqd,bhkd->bhqk', chosen, key_block.astype(jnp.float32), precision=PRECISE) * score_scale
        own_length = lax.optimization_barrier(jnp.sum(jnp.where(belongs, lengths[None, :], 0), axis=1))
        query_pos = own_length[:, None] - DRAFT_TOKENS + draft_row[None, :]
        key_pos = page_index[:, None] * PAGE_TOKENS + token_index[None, :]
        visible = (page_request < REQUEST_COUNT)[:, None, None] & (key_pos[:, None, :] <= query_pos[:, :, None])
        visible = visible[:, None, :, :]
        masked = jnp.where(visible, scores, NEGATIVE_FLOOR)
        page_max = lax.optimization_barrier(jnp.max(masked, axis=3))
        weights = jnp.where(visible, jnp.exp(masked - page_max[..., None]), 0.0)
        page_mass = lax.optimization_barrier(jnp.sum(weights, axis=3))
        rounded = lax.optimization_barrier(weights.astype(jnp.bfloat16)).astype(jnp.float32)
        page_out = jnp.einsum('bhqk,bhkd->bhqd', rounded, value_block.astype(jnp.float32), precision=PRECISE)
        request_max = lax.optimization_barrier(jnp.max(jnp.where(belongs[:, :, None, None], page_max[:, None], NEGATIVE_FLOOR), axis=0))
        new_maxima = jnp.maximum(maxima, request_max)
        carry_keep = jnp.exp(maxima - new_maxima)
        page_ref = jnp.einsum('br,rhq->bhq', onehot, new_maxima, precision=PRECISE)
        factor = jnp.exp(page_max - page_ref)
        running_totals = running_totals * carry_keep + jnp.einsum('br,bhq->rhq', onehot, page_mass * factor, precision=PRECISE)
        output_rows = output_rows * carry_keep[..., None] + jnp.einsum('br,bhqd->rhqd', onehot, page_out * factor[..., None], precision=PRECISE)
        return ((new_maxima, running_totals, output_rows), None)
    initial_state = (jnp.full((REQUEST_COUNT, KEY_VALUE_HEADS, query_matrix_rows), NEGATIVE_FLOOR, jnp.float32), jnp.zeros((REQUEST_COUNT, KEY_VALUE_HEADS, query_matrix_rows), jnp.float32), jnp.zeros((REQUEST_COUNT, KEY_VALUE_HEADS, query_matrix_rows, HEAD_SIZE), jnp.float32))
    (maxima, running_totals, output_rows), unused = lax.scan(visit, initial_state, (key_cache_blocks, value_cache_blocks, request_blocks, index_blocks))
    attended_output = (output_rows / running_totals[..., None]).reshape(REQUEST_COUNT, KEY_VALUE_HEADS, DRAFT_TOKENS, query_group_width, HEAD_SIZE).transpose(0, 2, 1, 3, 4).reshape(REQUEST_COUNT * DRAFT_TOKENS, QUERY_HEADS * HEAD_SIZE).astype(jnp.bfloat16)
    return jnp.dot(attended_output, out_weight, preferred_element_type=jnp.float32).astype(jnp.bfloat16)
```

```python
import functools
import math

import jax
import jax.numpy as jnp
from jax import lax
from jax.experimental import pallas as pl
from jax.experimental.pallas import tpu as pltpu
from jax.sharding import PartitionSpec as P

QUERY_HEADS = 64
KEY_VALUE_HEADS = 8
DRAFT_TOKENS = 16
GROUP = QUERY_HEADS // KEY_VALUE_HEADS

MASKED = -1e30
FLOOR = -0.5e30
MESH = pl.DeviceIdType.MESH


def attend(
    request_ref, page_ref, length_ref, q_ref, k_hbm, v_hbm, o_ref, stat_ref,
    q_rows, k_buf, v_buf, s_buf, lane_max, row_max, mass, acc, k_sem, v_sem,
):
    slots, page_tokens, head_dim = k_buf.shape
    requests = q_ref.shape[0]
    rows = q_rows.shape[1]
    per_owner = o_ref.shape[1]
    block = slots // k_sem.shape[0]
    scale2 = math.log2(math.e) / math.sqrt(head_dim)

    for b in range(slots // block):
        part = pl.ds(b * block, block)
        pltpu.make_async_copy(k_hbm.at[part, 0], k_buf.at[part], k_sem.at[b]).start()
    for b in range(slots // block):
        part = pl.ds(b * block, block)
        pltpu.make_async_copy(v_hbm.at[part, 0], v_buf.at[part], v_sem.at[b]).start()

    for r in range(requests):
        for h in range(GROUP):
            q_rows[r, h * DRAFT_TOKENS:(h + 1) * DRAFT_TOKENS, :] = q_ref[r, :, h * head_dim:(h + 1) * head_dim]
    lane_max[...] = jnp.full(lane_max.shape, FLOOR, jnp.float32)
    mass[...] = jnp.zeros(mass.shape, jnp.float32)
    acc[...] = jnp.zeros(acc.shape, jnp.float32)
    ahead = lax.broadcasted_iota(jnp.int32, (DRAFT_TOKENS, page_tokens), 1) - lax.broadcasted_iota(
        jnp.int32, (DRAFT_TOKENS, page_tokens), 0
    )

    def score(b, carry):
        part = pl.ds(b * block, block)
        pltpu.make_async_copy(k_hbm.at[part, 0], k_buf.at[part], k_sem.at[b]).wait()
        for u in range(block):
            slot = b * block + u
            r = request_ref[slot]
            known = jnp.minimum(r, requests - 1)
            limit = length_ref[known] - DRAFT_TOKENS - page_ref[slot] * page_tokens
            s = lax.dot_general(
                q_rows[known], k_buf[slot], (((1,), (1,)), ((), ())), preferred_element_type=jnp.float32
            )
            visible = ahead <= limit
            for h in range(GROUP):
                at = slice(h * DRAFT_TOKENS, (h + 1) * DRAFT_TOKENS)
                masked = jnp.where(visible, s[at], MASKED)
                s_buf[slot, at, :] = masked
                folded = jnp.maximum(masked[:, :head_dim], masked[:, head_dim:])
                lane_max[r, at, :] = jnp.maximum(lane_max[r, at, :], folded)
        return carry

    lax.fori_loop(0, slots // block, score, 0)

    for r in range(requests):
        row_max[r] = jnp.broadcast_to(jnp.max(lane_max[r], axis=1, keepdims=True), (rows, head_dim))
    row_max[requests] = jnp.zeros((rows, head_dim), jnp.float32)

    def weigh(b, carry):
        part = pl.ds(b * block, block)
        pltpu.make_async_copy(v_hbm.at[part, 0], v_buf.at[part], v_sem.at[b]).wait()
        for u in range(block):
            slot = b * block + u
            r = request_ref[slot]
            reference = row_max[r]
            left = jnp.exp2((s_buf[slot, :, :head_dim] - reference) * scale2)
            right = jnp.exp2((s_buf[slot, :, head_dim:] - reference) * scale2)
            mass[r] += left + right
            weights = jnp.concatenate([left, right], axis=1).astype(jnp.bfloat16)
            acc[r] += jnp.dot(weights, v_buf[slot], preferred_element_type=jnp.float32)
        return carry

    lax.fori_loop(0, slots // block, weigh, 0)

    lane = lax.broadcasted_iota(jnp.int32, (rows, head_dim), 1)
    row = lax.broadcasted_iota(jnp.int32, (rows, head_dim), 0)
    diagonal = lane % DRAFT_TOKENS == row % DRAFT_TOKENS
    piece = lane // DRAFT_TOKENS
    for a in range(requests // per_owner):
        packed = jnp.zeros((rows, head_dim), jnp.float32)
        for i in range(per_owner):
            r = a * per_owner + i
            total = jnp.sum(mass[r], axis=1, keepdims=True)
            packed = jnp.where(piece == i, row_max[r], packed)
            packed = jnp.where(piece == per_owner + i, jnp.broadcast_to(total, (rows, head_dim)), packed)
        packed = jnp.where(diagonal, packed, 0.0)
        for h in range(GROUP):
            at = slice(h * DRAFT_TOKENS, (h + 1) * DRAFT_TOKENS)
            stat_ref[a * GROUP + h] = jnp.sum(packed[at], axis=0, keepdims=True)
            for i in range(per_owner):
                o_ref[a * GROUP + h, i] = acc[a * per_owner + i, at, :].astype(jnp.bfloat16)


def exchange(
    n_ctx, n_kvh, o_ref, stat_ref, w_ref, out_ref,
    o_in, stat_in, att, share, o_send, o_recv, t_send, t_recv, a_send, a_recv, p_send, p_recv,
):
    c = lax.axis_index("ctx")
    k = lax.axis_index("kvh")
    per_owner, tokens, head_dim = o_ref.shape[1:]
    scale2 = math.log2(math.e) / math.sqrt(head_dim)

    def ctx_peer(i):
        return lax.rem(c + i, n_ctx)

    def kvh_peer(i):
        return lax.rem(k + i, n_kvh)

    barrier = pltpu.get_barrier_semaphore()

    def greet_ctx(i, carry):
        pl.semaphore_signal(barrier, inc=1, device_id=(ctx_peer(i), k), device_id_type=MESH)
        return carry

    def greet_kvh(i, carry):
        pl.semaphore_signal(barrier, inc=1, device_id=(c, kvh_peer(i)), device_id_type=MESH)
        return carry

    lax.fori_loop(1, n_ctx, greet_ctx, 0)
    lax.fori_loop(1, n_kvh, greet_kvh, 0)
    pl.semaphore_wait(barrier, n_ctx + n_kvh - 2)

    def stat_copy(i):
        return pltpu.make_async_remote_copy(
            src_ref=stat_ref.at[ctx_peer(i)], dst_ref=stat_in.at[c],
            send_sem=t_send.at[i], recv_sem=t_recv.at[i],
            device_id=(ctx_peer(i), k), device_id_type=MESH,
        )

    def o_copy(i):
        return pltpu.make_async_remote_copy(
            src_ref=o_ref.at[ctx_peer(i)], dst_ref=o_in.at[c],
            send_sem=o_send.at[i], recv_sem=o_recv.at[i],
            device_id=(ctx_peer(i), k), device_id_type=MESH,
        )

    def att_copy(i):
        return pltpu.make_async_remote_copy(
            src_ref=att.at[c], dst_ref=att.at[c],
            send_sem=a_send.at[i], recv_sem=a_recv.at[i],
            device_id=(ctx_peer(i), k), device_id_type=MESH,
        )

    def share_copy(i):
        return pltpu.make_async_remote_copy(
            src_ref=share.at[kvh_peer(i)], dst_ref=out_ref.at[k],
            send_sem=p_send.at[i], recv_sem=p_recv.at[i],
            device_id=(c, kvh_peer(i)), device_id_type=MESH,
        )

    def start_partials(i, carry):
        stat_copy(i).start()
        o_copy(i).start()
        return carry

    lax.fori_loop(1, n_ctx, start_partials, 0)
    stat_in[c] = stat_ref[c]
    o_in[c] = o_ref[c]

    def wait_stats(i, carry):
        stat_copy(i).wait_recv()
        return carry

    def wait_partials(i, carry):
        o_copy(i).wait_recv()
        return carry

    lax.fori_loop(1, n_ctx, wait_stats, 0)
    stats = stat_in[...].reshape(n_ctx, head_dim)
    span = per_owner * tokens
    joined = jnp.max(stats, axis=0, keepdims=True)
    factor = jnp.exp2((stats - joined) * scale2)
    masses = pltpu.roll(stats, head_dim - span, 1)
    lane = lax.broadcasted_iota(jnp.int32, stats.shape, 1)
    factor = jnp.where(lane < span, factor, 0.0)
    total = jnp.sum(factor * masses, axis=0, keepdims=True)
    total = jnp.where(lane[:1] < span, total, 1.0)
    factor = (factor / total).T
    lax.fori_loop(1, n_ctx, wait_partials, 0)
    attended = jnp.zeros((span, head_dim), jnp.float32)
    for s in range(n_ctx):
        attended += factor[:span, s:s + 1] * o_in[s].reshape(span, head_dim).astype(jnp.float32)
    att[c] = attended.astype(jnp.bfloat16).reshape(per_owner, tokens, head_dim)

    def start_att(i, carry):
        att_copy(i).start()
        return carry

    def wait_att(i, carry):
        att_copy(i).wait_recv()
        return carry

    lax.fori_loop(1, n_ctx, start_att, 0)
    lax.fori_loop(1, n_ctx, wait_att, 0)

    heads = w_ref.shape[0] // head_dim
    groups = n_ctx // heads
    operand = jnp.concatenate(
        [
            jnp.concatenate([att[a * heads + h].reshape(span, head_dim) for a in range(groups)], axis=0)
            for h in range(heads)
        ],
        axis=1,
    )
    product = jnp.dot(operand, w_ref[...], preferred_element_type=jnp.float32).astype(jnp.bfloat16)
    part = share.shape[1]
    for d in range(n_kvh):
        share[d] = product[d * part:(d + 1) * part]

    def start_share(i, carry):
        share_copy(i).start()
        return carry

    def finish_share(i, carry):
        share_copy(i).wait()
        return carry

    def finish_ctx(i, carry):
        stat_copy(i).wait_send()
        o_copy(i).wait_send()
        att_copy(i).wait_send()
        return carry

    lax.fori_loop(1, n_kvh, start_share, 0)
    out_ref[k] = share[k]
    lax.fori_loop(1, n_ctx, finish_ctx, 0)
    lax.fori_loop(1, n_kvh, finish_share, 0)


def per_device(n_ctx, n_kvh, queries, keys, values, out_weight, lengths, slot_request, slot_page):
    requests = queries.shape[0]
    slots, _, page_tokens, head_dim = keys.shape
    rows = DRAFT_TOKENS * GROUP
    per_owner = requests * GROUP // n_ctx
    owned = (n_ctx, per_owner, DRAFT_TOKENS, head_dim)
    smem = pl.BlockSpec(memory_space=pltpu.SMEM)
    vmem = pl.BlockSpec(memory_space=pltpu.VMEM)
    hbm = pl.BlockSpec(memory_space=pl.ANY)
    blocks = slots // 4
    partial, stats = pl.pallas_call(
        attend,
        out_shape=(
            jax.ShapeDtypeStruct(owned, jnp.bfloat16),
            jax.ShapeDtypeStruct((n_ctx, 1, head_dim), jnp.float32),
        ),
        in_specs=[smem, smem, smem, vmem, hbm, hbm],
        out_specs=(vmem, vmem),
        scratch_shapes=[
            pltpu.VMEM((requests, rows, head_dim), jnp.bfloat16),
            pltpu.VMEM((slots, page_tokens, head_dim), jnp.bfloat16),
            pltpu.VMEM((slots, page_tokens, head_dim), jnp.bfloat16),
            pltpu.VMEM((slots, rows, page_tokens), jnp.float32),
            pltpu.VMEM((requests + 1, rows, head_dim), jnp.float32),
            pltpu.VMEM((requests + 1, rows, head_dim), jnp.float32),
            pltpu.VMEM((requests + 1, rows, head_dim), jnp.float32),
            pltpu.VMEM((requests + 1, rows, head_dim), jnp.float32),
            pltpu.SemaphoreType.DMA((blocks,)),
            pltpu.SemaphoreType.DMA((blocks,)),
        ],
        compiler_params=pltpu.CompilerParams(vmem_limit_bytes=40 << 20),
        name="attend",
    )(slot_request, slot_page, lengths, queries, keys, values)

    total_rows = requests * DRAFT_TOKENS
    columns = out_weight.shape[1]
    shares = pl.pallas_call(
        functools.partial(exchange, n_ctx, n_kvh),
        out_shape=jax.ShapeDtypeStruct((n_kvh, total_rows // n_kvh, columns), jnp.bfloat16),
        in_specs=[vmem, vmem, vmem],
        out_specs=vmem,
        scratch_shapes=[
            pltpu.VMEM(owned, jnp.bfloat16),
            pltpu.VMEM((n_ctx, 1, head_dim), jnp.float32),
            pltpu.VMEM(owned, jnp.bfloat16),
            pltpu.VMEM((n_kvh, total_rows // n_kvh, columns), jnp.bfloat16),
        ]
        + [pltpu.SemaphoreType.DMA((n_ctx,))] * 6
        + [pltpu.SemaphoreType.DMA((n_kvh,))] * 2,
        compiler_params=pltpu.CompilerParams(
            collective_id=0, has_side_effects=True, vmem_limit_bytes=32 << 20
        ),
        name="exchange",
    )(partial, stats, out_weight)
    return jnp.sum(shares.astype(jnp.float32), axis=0).astype(jnp.bfloat16)


def solution(mesh):
    placed = (
        P(None, None, "kvh"),
        P("ctx", "kvh", None, None),
        P("ctx", "kvh", None, None),
        P("kvh", "ctx"),
        P(),
        P("ctx"),
        P("ctx"),
    )
    return jax.shard_map(
        functools.partial(per_device, mesh.shape["ctx"], mesh.shape["kvh"]),
        mesh=mesh, in_specs=placed, out_specs=P("kvh", "ctx"), check_vma=False,
    )
```

```python
import functools
import math

import jax
import jax.numpy as jnp
from jax import lax
from jax.experimental import pallas as pl
from jax.experimental.pallas import tpu as pltpu
from jax.sharding import PartitionSpec as P

QUERY_HEADS = 64
KEY_VALUE_HEADS = 8
DRAFT_TOKENS = 16
GROUP = QUERY_HEADS // KEY_VALUE_HEADS

MASKED = -1e30
FLOOR = -0.5e30
MESH = pl.DeviceIdType.MESH


def step(
    n_ctx, n_kvh, block,
    request_hbm, page_hbm, length_hbm, q_hbm, k_hbm, v_hbm, w_hbm, out_ref,
    request_ref, page_ref, length_ref, before_ref, last_ref,
    q_in, q_rows, k_buf, v_buf, w_buf, s_buf, lane_max, row_max, mass, acc,
    o_out, stat_out, o_in, stat_in, att, share,
    small_sem, k_sem, v_sem, o_send, o_recv, t_send, t_recv, z_send, z_recv, x_send, x_recv, p_send, p_recv,
):
    c = lax.axis_index("ctx")
    k = lax.axis_index("kvh")
    slots, page_tokens, head_dim = k_buf.shape
    requests, rows = q_rows.shape[:2]
    per_owner, tokens = o_out.shape[1:3]
    heads = rows // tokens
    groups = n_ctx // heads
    blocks = slots // block
    scale2 = math.log2(math.e) / math.sqrt(head_dim)
    x, z = c // heads, lax.rem(c, heads)

    def fetch(source, target, sem):
        return pltpu.make_async_copy(source, target, sem)

    def k_copy(b):
        part = pl.ds(b * block, block)
        return fetch(k_hbm.at[part, 0], k_buf.at[part], k_sem.at[b])

    def v_copy(b):
        part = pl.ds(b * block, block)
        return fetch(v_hbm.at[part, 0], v_buf.at[part], v_sem.at[b])

    first = [
        fetch(request_hbm, request_ref, small_sem.at[0]),
        fetch(page_hbm, page_ref, small_sem.at[1]),
        fetch(length_hbm, length_ref, small_sem.at[2]),
        fetch(q_hbm, q_in, small_sem.at[3]),
    ]
    w_copy = fetch(w_hbm, w_buf, small_sem.at[4])
    for copy in first:
        copy.start()
    for b in range(blocks):
        k_copy(b).start()
    for b in range(blocks):
        v_copy(b).start()
    w_copy.start()

    def ctx_device(j, i):
        return lax.rem(x + j, groups) * heads + lax.rem(z + i, heads)

    def kvh_device(i):
        return lax.rem(k + i, n_kvh)

    barrier = pltpu.get_barrier_semaphore()

    def greet_ctx(i, carry):
        pl.semaphore_signal(barrier, inc=1, device_id=(lax.rem(c + i, n_ctx), k), device_id_type=MESH)
        return carry

    def greet_kvh(i, carry):
        pl.semaphore_signal(barrier, inc=1, device_id=(c, kvh_device(i)), device_id_type=MESH)
        return carry

    lax.fori_loop(1, n_ctx, greet_ctx, 0)
    lax.fori_loop(1, n_kvh, greet_kvh, 0)

    lane_max[slots] = jnp.full((rows, head_dim), FLOOR, jnp.float32)
    mass[slots] = jnp.zeros((rows, head_dim), jnp.float32)
    acc[slots] = jnp.zeros((rows, head_dim), jnp.float32)
    ahead = lax.broadcasted_iota(jnp.int32, (tokens, page_tokens), 1) - lax.broadcasted_iota(
        jnp.int32, (tokens, page_tokens), 0
    )
    for copy in first:
        copy.wait()
    for r in range(requests):
        for h in range(heads):
            q_rows[r, h * tokens:(h + 1) * tokens, :] = q_in[r, :, h * head_dim:(h + 1) * head_dim]

    def score(b, last):
        k_copy(b).wait()
        for u in range(block):
            slot = b * block + u
            r = request_ref[slot]
            known = jnp.minimum(r, requests - 1)
            limit = length_ref[known] - tokens - page_ref[slot] * page_tokens
            limit = jnp.where(r < requests, limit, -page_tokens)
            before = jnp.int32(slots)
            for n in range(requests):
                before = jnp.where(r == n, last[n], before)
            last = tuple(jnp.where(r == n, slot, last[n]) for n in range(requests))
            before_ref[slot] = before
            s = lax.dot_general(
                q_rows[known], k_buf[slot], (((1,), (1,)), ((), ())), preferred_element_type=jnp.float32
            )
            visible = ahead <= limit
            for h in range(heads):
                at = slice(h * tokens, (h + 1) * tokens)
                masked = jnp.where(visible, s[at], MASKED)
                s_buf[slot, at, :] = masked
                folded = jnp.maximum(masked[:, :head_dim], masked[:, head_dim:])
                lane_max[slot, at, :] = jnp.maximum(lane_max[before, at, :], folded)
        return last

    last = lax.fori_loop(0, blocks, score, (jnp.int32(slots),) * requests)

    for r in range(requests):
        last_ref[r] = last[r]
        row_max[r] = jnp.broadcast_to(jnp.max(lane_max[last[r]], axis=1, keepdims=True), (rows, head_dim))
    row_max[requests] = jnp.zeros((rows, head_dim), jnp.float32)

    def weigh(b, carry):
        v_copy(b).wait()
        for u in range(block):
            slot = b * block + u
            before = before_ref[slot]
            reference = row_max[request_ref[slot]]
            left = jnp.exp2((s_buf[slot, :, :head_dim] - reference) * scale2)
            right = jnp.exp2((s_buf[slot, :, head_dim:] - reference) * scale2)
            mass[slot] = mass[before] + (left + right)
            weights = jnp.concatenate([left, right], axis=1).astype(jnp.bfloat16)
            acc[slot] = acc[before] + jnp.dot(weights, v_buf[slot], preferred_element_type=jnp.float32)
        return carry

    lax.fori_loop(0, blocks, weigh, 0)

    def stat_copy(j, i):
        device, n = ctx_device(j, i), j * heads + i
        return pltpu.make_async_remote_copy(
            src_ref=stat_out.at[device], dst_ref=stat_in.at[c], send_sem=t_send.at[n], recv_sem=t_recv.at[n],
            device_id=(device, k), device_id_type=MESH,
        )

    def o_copy(j, i):
        device, n = ctx_device(j, i), j * heads + i
        return pltpu.make_async_remote_copy(
            src_ref=o_out.at[device], dst_ref=o_in.at[c], send_sem=o_send.at[n], recv_sem=o_recv.at[n],
            device_id=(device, k), device_id_type=MESH,
        )

    def z_copy(i):
        return pltpu.make_async_remote_copy(
            src_ref=att.at[c], dst_ref=att.at[c], send_sem=z_send.at[i], recv_sem=z_recv.at[i],
            device_id=(ctx_device(0, i), k), device_id_type=MESH,
        )

    def x_copy(j, i):
        source, n = x * heads + lax.rem(z + heads - i, heads), j * heads + i
        return pltpu.make_async_remote_copy(
            src_ref=att.at[source], dst_ref=att.at[source], send_sem=x_send.at[n], recv_sem=x_recv.at[n],
            device_id=(ctx_device(j, 0), k), device_id_type=MESH,
        )

    def share_copy(i):
        return pltpu.make_async_remote_copy(
            src_ref=share.at[kvh_device(i)], dst_ref=out_ref.at[k], send_sem=p_send.at[i], recv_sem=p_recv.at[i],
            device_id=(c, kvh_device(i)), device_id_type=MESH,
        )

    pl.semaphore_wait(barrier, n_ctx + n_kvh - 2)

    lane = lax.broadcasted_iota(jnp.int32, (rows, head_dim), 1)
    row = lax.broadcasted_iota(jnp.int32, (rows, head_dim), 0)
    diagonal = lane % tokens == row % tokens
    piece = lane // tokens

    def hand_out(n, carry):
        j = groups - 1 - n
        a = lax.rem(x + j, groups)
        packed = jnp.zeros((rows, head_dim), jnp.float32)
        for i in range(per_owner):
            r = a * per_owner + i
            entry = last_ref[r]
            total = jnp.sum(mass[entry], axis=1, keepdims=True)
            packed = jnp.where(piece == i, row_max[r], packed)
            packed = jnp.where(piece == per_owner + i, jnp.broadcast_to(total, (rows, head_dim)), packed)
            for h in range(heads):
                at = slice(h * tokens, (h + 1) * tokens)
                o_out[a * heads + h, i] = acc[entry, at, :].astype(jnp.bfloat16)
        packed = jnp.where(diagonal, packed, 0.0)
        for h in range(heads):
            at = slice(h * tokens, (h + 1) * tokens)
            stat_out[a * heads + h] = jnp.sum(packed[at], axis=0, keepdims=True)

        def start(i, inner):
            stat_copy(j, i).start()
            o_copy(j, i).start()
            return inner

        lax.fori_loop(jnp.where(j == 0, 1, 0), heads, start, 0)
        return carry

    lax.fori_loop(0, groups, hand_out, 0)
    stat_in[c] = stat_out[c]
    o_in[c] = o_out[c]

    def each_ctx(act):
        def visit(n, carry):
            act(n // heads, lax.rem(n, heads))
            return carry

        lax.fori_loop(1, n_ctx, visit, 0)

    each_ctx(lambda j, i: stat_copy(j, i).wait_recv())
    stats = stat_in[...].reshape(n_ctx, head_dim)
    span = per_owner * tokens
    joined = jnp.max(stats, axis=0, keepdims=True)
    factor = jnp.exp2((stats - joined) * scale2)
    masses = pltpu.roll(stats, head_dim - span, 1)
    column = lax.broadcasted_iota(jnp.int32, stats.shape, 1)
    factor = jnp.where(column < span, factor, 0.0)
    total = jnp.sum(factor * masses, axis=0, keepdims=True)
    total = jnp.where(column[:1] < span, total, 1.0)
    factor = (factor / total).T
    each_ctx(lambda j, i: o_copy(j, i).wait_recv())
    attended = jnp.zeros((span, head_dim), jnp.float32)
    for s in range(n_ctx):
        attended += factor[:span, s:s + 1] * o_in[s].reshape(span, head_dim).astype(jnp.float32)
    att[c] = attended.astype(jnp.bfloat16).reshape(per_owner, tokens, head_dim)

    near_first = [i for pair in zip(range(1, heads // 2), range(heads - 1, heads // 2, -1)) for i in pair] + [heads // 2]
    beside = [1, groups - 1] + list(range(2, groups - 1))
    for i in near_first:
        z_copy(i).start()
    for j in beside:
        x_copy(j, 0).start()
    for i in near_first:
        z_copy(i).wait_recv()
        for j in beside:
            x_copy(j, i).start()
    for i in [0] + near_first:
        for j in beside:
            x_copy(j, i).wait_recv()

    w_copy.wait()
    operand = jnp.concatenate(
        [
            jnp.concatenate([att[a * heads + h].reshape(span, head_dim) for a in range(groups)], axis=0)
            for h in range(heads)
        ],
        axis=1,
    )
    product = jnp.dot(operand, w_buf[...], preferred_element_type=jnp.float32).astype(jnp.bfloat16)
    part = share.shape[1]
    for d in range(n_kvh):
        share[d] = product[d * part:(d + 1) * part]

    def start_share(i, carry):
        share_copy(i).start()
        return carry

    def finish_share(i, carry):
        share_copy(i).wait()
        return carry

    lax.fori_loop(1, n_kvh, start_share, 0)
    out_ref[k] = share[k]

    def settle(j, i):
        stat_copy(j, i).wait_send()
        o_copy(j, i).wait_send()

    each_ctx(settle)
    for i in near_first:
        z_copy(i).wait_send()
    for i in [0] + near_first:
        for j in beside:
            x_copy(j, i).wait_send()
    lax.fori_loop(1, n_kvh, finish_share, 0)


def per_device(n_ctx, n_kvh, queries, keys, values, out_weight, lengths, slot_request, slot_page):
    requests = queries.shape[0]
    slots, _, page_tokens, head_dim = keys.shape
    rows = DRAFT_TOKENS * GROUP
    per_owner = requests * GROUP // n_ctx
    owned = (n_ctx, per_owner, DRAFT_TOKENS, head_dim)
    total_rows = requests * DRAFT_TOKENS
    columns = out_weight.shape[1]
    block = 4
    blocks = slots // block
    shared = (n_kvh, total_rows // n_kvh, columns)
    shares = pl.pallas_call(
        functools.partial(step, n_ctx, n_kvh, block),
        out_shape=jax.ShapeDtypeStruct(shared, jnp.bfloat16),
        in_specs=[pl.BlockSpec(memory_space=pltpu.HBM)] * 7,
        out_specs=pl.BlockSpec(memory_space=pltpu.VMEM),
        scratch_shapes=[
            pltpu.SMEM((slots,), jnp.int32),
            pltpu.SMEM((slots,), jnp.int32),
            pltpu.SMEM((requests,), jnp.int32),
            pltpu.SMEM((slots,), jnp.int32),
            pltpu.SMEM((requests,), jnp.int32),
            pltpu.VMEM(queries.shape, jnp.bfloat16),
            pltpu.VMEM((requests, rows, head_dim), jnp.bfloat16),
            pltpu.VMEM((slots, page_tokens, head_dim), jnp.bfloat16),
            pltpu.VMEM((slots, page_tokens, head_dim), jnp.bfloat16),
            pltpu.VMEM(out_weight.shape, jnp.bfloat16),
            pltpu.VMEM((slots, rows, page_tokens), jnp.float32),
            pltpu.VMEM((slots + 1, rows, head_dim), jnp.float32),
            pltpu.VMEM((requests + 1, rows, head_dim), jnp.float32),
            pltpu.VMEM((slots + 1, rows, head_dim), jnp.float32),
            pltpu.VMEM((slots + 1, rows, head_dim), jnp.float32),
            pltpu.VMEM(owned, jnp.bfloat16),
            pltpu.VMEM((n_ctx, 1, head_dim), jnp.float32),
            pltpu.VMEM(owned, jnp.bfloat16),
            pltpu.VMEM((n_ctx, 1, head_dim), jnp.float32),
            pltpu.VMEM(owned, jnp.bfloat16),
            pltpu.VMEM(shared, jnp.bfloat16),
            pltpu.SemaphoreType.DMA((5,)),
            pltpu.SemaphoreType.DMA((blocks,)),
            pltpu.SemaphoreType.DMA((blocks,)),
        ]
        + [pltpu.SemaphoreType.DMA((n_ctx,))] * 4
        + [pltpu.SemaphoreType.DMA((GROUP,))] * 2
        + [pltpu.SemaphoreType.DMA((n_ctx,))] * 2
        + [pltpu.SemaphoreType.DMA((n_kvh,))] * 2,
        compiler_params=pltpu.CompilerParams(
            collective_id=0, has_side_effects=True, vmem_limit_bytes=60 << 20
        ),
        name="step",
    )(slot_request, slot_page, lengths, queries, keys, values, out_weight)
    return jnp.sum(shares.astype(jnp.float32), axis=0).astype(jnp.bfloat16)


def solution(mesh):
    placed = (
        P(None, None, "kvh"),
        P("ctx", "kvh", None, None),
        P("ctx", "kvh", None, None),
        P("kvh", "ctx"),
        P(),
        P("ctx"),
        P("ctx"),
    )
    return jax.shard_map(
        functools.partial(per_device, mesh.shape["ctx"], mesh.shape["kvh"]),
        mesh=mesh, in_specs=placed, out_specs=P("kvh", "ctx"), check_vma=False,
    )
```

```python
import functools
import math

import jax
import jax.numpy as jnp
from jax import lax
from jax.experimental import pallas as pl
from jax.experimental.pallas import tpu as pltpu
from jax.sharding import PartitionSpec as P

QUERY_HEADS = 64
KEY_VALUE_HEADS = 8
DRAFT_TOKENS = 16
GROUP = QUERY_HEADS // KEY_VALUE_HEADS

MASKED = -1e30
FLOOR = -0.5e30
MESH = pl.DeviceIdType.MESH


def step(
    n_ctx, n_kvh, block,
    request_hbm, page_hbm, length_hbm, q_hbm, k_hbm, v_hbm, w_hbm, out_ref,
    request_ref, page_ref, length_ref, last_ref,
    q_in, q_rows, k_buf, v_buf, w_buf, ahead, top, mass, acc,
    o_out, stat_out, o_in, stat_in, att, share, share_in,
    small_sem, k_sem, v_sem, o_send, o_recv, t_send, t_recv, z_send, z_recv, x_send, x_recv, p_send, p_recv,
):
    c = lax.axis_index("ctx")
    k = lax.axis_index("kvh")
    slots, page_tokens, head_dim = k_buf.shape
    requests, rows = q_rows.shape[:2]
    per_owner, tokens = o_out.shape[1:3]
    heads = rows // tokens
    groups = n_ctx // heads
    blocks = slots // block
    scale2 = math.log2(math.e) / math.sqrt(head_dim)
    x, z = c // heads, lax.rem(c, heads)

    def fetch(source, target, sem):
        return pltpu.make_async_copy(source, target, sem)

    def k_copy(b):
        part = pl.ds(b * block, block)
        return fetch(k_hbm.at[part, 0], k_buf.at[part], k_sem.at[b])

    def v_copy(b):
        part = pl.ds(b * block, block)
        return fetch(v_hbm.at[part, 0], v_buf.at[part], v_sem.at[b])

    first = [
        fetch(request_hbm, request_ref, small_sem.at[0]),
        fetch(page_hbm, page_ref, small_sem.at[1]),
        fetch(length_hbm, length_ref, small_sem.at[2]),
        fetch(q_hbm, q_in, small_sem.at[3]),
    ]
    w_copy = fetch(w_hbm, w_buf, small_sem.at[4])
    for copy in first:
        copy.start()
    for b in range(blocks):
        k_copy(b).start()
        v_copy(b).start()
    w_copy.start()

    def ctx_device(j, i):
        return lax.rem(x + j, groups) * heads + lax.rem(z + i, heads)

    def kvh_device(i):
        return lax.rem(k + i, n_kvh)

    barrier = pltpu.get_barrier_semaphore()

    def greet_ctx(i, carry):
        pl.semaphore_signal(barrier, inc=1, device_id=(lax.rem(c + i, n_ctx), k), device_id_type=MESH)
        return carry

    def greet_kvh(i, carry):
        pl.semaphore_signal(barrier, inc=1, device_id=(c, kvh_device(i)), device_id_type=MESH)
        return carry

    lax.fori_loop(1, n_ctx, greet_ctx, 0)
    lax.fori_loop(1, n_kvh, greet_kvh, 0)

    top[slots] = jnp.full((1, rows), FLOOR, jnp.float32)
    mass[slots] = jnp.zeros((1, rows), jnp.float32)
    acc[slots] = jnp.zeros((head_dim, rows), jnp.float32)
    ahead[...] = lax.broadcasted_iota(jnp.int32, (page_tokens, rows), 0) - lax.rem(
        lax.broadcasted_iota(jnp.int32, (page_tokens, rows), 1), tokens
    )
    for copy in first:
        copy.wait()
    for r in range(requests):
        for h in range(heads):
            q_rows[r, h * tokens:(h + 1) * tokens, :] = q_in[r, :, h * head_dim:(h + 1) * head_dim]

    def visit(b, last):
        k_copy(b).wait()
        v_copy(b).wait()
        part = [b * block + u for u in range(block)]
        befores, scores, peaks, masses, outs = [], [], [], [], []
        for slot in part:
            r = request_ref[slot]
            known = jnp.minimum(r, requests - 1)
            limit = length_ref[known] - tokens - page_ref[slot] * page_tokens
            limit = jnp.where(r < requests, limit, -page_tokens)
            before = jnp.int32(slots)
            for n in range(requests):
                before = jnp.where(r == n, last[n], before)
            last = tuple(jnp.where(r == n, slot, last[n]) for n in range(requests))
            befores.append(before)
            s = lax.dot_general(
                k_buf[slot], q_rows[known], (((1,), (1,)), ((), ())), preferred_element_type=jnp.float32
            )
            s = jnp.where(ahead[...] <= limit, s, MASKED)
            scores.append(s)
            peaks.append(jnp.maximum(jnp.max(s, axis=0, keepdims=True), FLOOR))
        for slot, s, peak in zip(part, scores, peaks):
            weights = jnp.exp2((s - peak) * scale2)
            masses.append(jnp.sum(weights, axis=0, keepdims=True))
            outs.append(lax.dot_general(
                v_buf[slot], weights.astype(jnp.bfloat16), (((0,), (0,)), ((), ())),
                preferred_element_type=jnp.float32,
            ))
        for slot, before, peak, page_mass, page_out in zip(part, befores, peaks, masses, outs):
            old = top[before]
            new = jnp.maximum(old, peak)
            keep = jnp.exp2((old - new) * scale2)
            gain = jnp.exp2((peak - new) * scale2)
            top[slot] = new
            mass[slot] = mass[before] * keep + page_mass * gain
            acc[slot] = acc[before] * keep + page_out * gain
        return last

    last = lax.fori_loop(0, blocks, visit, (jnp.int32(slots),) * requests)
    for r in range(requests):
        last_ref[r] = last[r]

    def stat_copy(j, i):
        device, n = ctx_device(j, i), j * heads + i
        return pltpu.make_async_remote_copy(
            src_ref=stat_out.at[device], dst_ref=stat_in.at[c], send_sem=t_send.at[n], recv_sem=t_recv.at[n],
            device_id=(device, k), device_id_type=MESH,
        )

    def o_copy(j, i):
        device, n = ctx_device(j, i), j * heads + i
        return pltpu.make_async_remote_copy(
            src_ref=o_out.at[device], dst_ref=o_in.at[c], send_sem=o_send.at[n], recv_sem=o_recv.at[n],
            device_id=(device, k), device_id_type=MESH,
        )

    def z_copy(i):
        return pltpu.make_async_remote_copy(
            src_ref=att.at[c], dst_ref=att.at[c], send_sem=z_send.at[i], recv_sem=z_recv.at[i],
            device_id=(ctx_device(0, i), k), device_id_type=MESH,
        )

    def x_copy(j, i):
        source, n = x * heads + lax.rem(z + heads - i, heads), j * heads + i
        return pltpu.make_async_remote_copy(
            src_ref=att.at[source], dst_ref=att.at[source], send_sem=x_send.at[n], recv_sem=x_recv.at[n],
            device_id=(ctx_device(j, 0), k), device_id_type=MESH,
        )

    def share_copy(i):
        return pltpu.make_async_remote_copy(
            src_ref=share.at[kvh_device(i)], dst_ref=share_in.at[k], send_sem=p_send.at[i], recv_sem=p_recv.at[i],
            device_id=(c, kvh_device(i)), device_id_type=MESH,
        )

    pl.semaphore_wait(barrier, n_ctx + n_kvh - 2)

    lane = lax.broadcasted_iota(jnp.int32, (8, rows), 1)
    kind = lax.broadcasted_iota(jnp.int32, (8, rows), 0)

    def hand_out(n, carry):
        j = groups - 1 - n
        a = lax.rem(x + j, groups)
        packed = jnp.zeros((8, rows), jnp.float32)
        for i in range(per_owner):
            entry = last_ref[a * per_owner + i]
            packed = jnp.where(kind == i, top[entry], packed)
            packed = jnp.where(kind == per_owner + i, mass[entry], packed)
            turned = acc[entry].T.astype(jnp.bfloat16)
            for h in range(heads):
                o_out[a * heads + h, i] = turned[h * tokens:(h + 1) * tokens]
        slanted = pltpu.roll(packed, 0, 1, stride=tokens, stride_axis=0)
        for h in range(heads):
            moved = pltpu.roll(slanted, (rows - h * tokens) % rows, 1)
            moved = jnp.where(lane // tokens == kind, moved, 0.0)
            stat_out[a * heads + h] = jnp.sum(moved, axis=0, keepdims=True)

        def start(i, inner):
            stat_copy(j, i).start()
            o_copy(j, i).start()
            return inner

        lax.fori_loop(jnp.where(j == 0, 1, 0), heads, start, 0)
        return carry

    lax.fori_loop(0, groups, hand_out, 0)
    stat_in[c] = stat_out[c]
    o_in[c] = o_out[c]

    def each_ctx(act):
        def visit(n, carry):
            act(n // heads, lax.rem(n, heads))
            return carry

        lax.fori_loop(1, n_ctx, visit, 0)

    each_ctx(lambda j, i: stat_copy(j, i).wait_recv())
    stats = stat_in[...].reshape(n_ctx, head_dim)
    span = per_owner * tokens
    joined = jnp.max(stats, axis=0, keepdims=True)
    factor = jnp.exp2((stats - joined) * scale2)
    masses = pltpu.roll(stats, head_dim - span, 1)
    column = lax.broadcasted_iota(jnp.int32, stats.shape, 1)
    factor = jnp.where(column < span, factor, 0.0)
    total = jnp.sum(factor * masses, axis=0, keepdims=True)
    total = jnp.where(column[:1] < span, total, 1.0)
    factor = (factor / total).T
    each_ctx(lambda j, i: o_copy(j, i).wait_recv())
    attended = jnp.zeros((span, head_dim), jnp.float32)
    for s in range(n_ctx):
        attended += factor[:span, s:s + 1] * o_in[s].reshape(span, head_dim).astype(jnp.float32)
    att[c] = attended.astype(jnp.bfloat16).reshape(per_owner, tokens, head_dim)

    near_first = [i for pair in zip(range(1, heads // 2), range(heads - 1, heads // 2, -1)) for i in pair] + [heads // 2]
    beside = [1, groups - 1] + list(range(2, groups - 1))
    for i in near_first:
        z_copy(i).start()
    for j in beside:
        x_copy(j, 0).start()
    for i in near_first:
        z_copy(i).wait_recv()
        for j in beside:
            x_copy(j, i).start()
    for i in [0] + near_first:
        for j in beside:
            x_copy(j, i).wait_recv()

    w_copy.wait()
    operand = jnp.concatenate(
        [
            jnp.concatenate([att[a * heads + h].reshape(span, head_dim) for a in range(groups)], axis=0)
            for h in range(heads)
        ],
        axis=1,
    )
    product = jnp.dot(operand, w_buf[...], preferred_element_type=jnp.float32).astype(jnp.bfloat16)
    part = share.shape[1]
    for d in range(n_kvh):
        share[d] = product[d * part:(d + 1) * part]

    def start_share(i, carry):
        share_copy(i).start()
        return carry

    def finish_share(i, carry):
        share_copy(i).wait()
        return carry

    lax.fori_loop(1, n_kvh, start_share, 0)
    share_in[k] = share[k]

    def settle(j, i):
        stat_copy(j, i).wait_send()
        o_copy(j, i).wait_send()

    each_ctx(settle)
    for i in near_first:
        z_copy(i).wait_send()
    for i in [0] + near_first:
        for j in beside:
            x_copy(j, i).wait_send()
    lax.fori_loop(1, n_kvh, finish_share, 0)
    summed = share_in[0].astype(jnp.float32)
    for d in range(1, n_kvh):
        summed += share_in[d].astype(jnp.float32)
    out_ref[...] = summed.astype(jnp.bfloat16)


def per_device(n_ctx, n_kvh, queries, keys, values, out_weight, lengths, slot_request, slot_page):
    requests = queries.shape[0]
    slots, _, page_tokens, head_dim = keys.shape
    rows = DRAFT_TOKENS * GROUP
    per_owner = requests * GROUP // n_ctx
    owned = (n_ctx, per_owner, DRAFT_TOKENS, head_dim)
    total_rows = requests * DRAFT_TOKENS
    columns = out_weight.shape[1]
    block = 16
    blocks = slots // block
    shared = (n_kvh, total_rows // n_kvh, columns)
    return pl.pallas_call(
        functools.partial(step, n_ctx, n_kvh, block),
        out_shape=jax.ShapeDtypeStruct(shared[1:], jnp.bfloat16),
        in_specs=[pl.BlockSpec(memory_space=pltpu.HBM)] * 7,
        out_specs=pl.BlockSpec(memory_space=pltpu.VMEM),
        scratch_shapes=[
            pltpu.SMEM((slots,), jnp.int32),
            pltpu.SMEM((slots,), jnp.int32),
            pltpu.SMEM((requests,), jnp.int32),
            pltpu.SMEM((requests,), jnp.int32),
            pltpu.VMEM(queries.shape, jnp.bfloat16),
            pltpu.VMEM((requests, rows, head_dim), jnp.bfloat16),
            pltpu.VMEM((slots, page_tokens, head_dim), jnp.bfloat16),
            pltpu.VMEM((slots, page_tokens, head_dim), jnp.bfloat16),
            pltpu.VMEM(out_weight.shape, jnp.bfloat16),
            pltpu.VMEM((page_tokens, rows), jnp.int32),
            pltpu.VMEM((slots + 1, 1, rows), jnp.float32),
            pltpu.VMEM((slots + 1, 1, rows), jnp.float32),
            pltpu.VMEM((slots + 1, head_dim, rows), jnp.float32),
            pltpu.VMEM(owned, jnp.bfloat16),
            pltpu.VMEM((n_ctx, 1, head_dim), jnp.float32),
            pltpu.VMEM(owned, jnp.bfloat16),
            pltpu.VMEM((n_ctx, 1, head_dim), jnp.float32),
            pltpu.VMEM(owned, jnp.bfloat16),
            pltpu.VMEM(shared, jnp.bfloat16),
            pltpu.VMEM(shared, jnp.bfloat16),
            pltpu.SemaphoreType.DMA((5,)),
            pltpu.SemaphoreType.DMA((blocks,)),
            pltpu.SemaphoreType.DMA((blocks,)),
        ]
        + [pltpu.SemaphoreType.DMA((n_ctx,))] * 4
        + [pltpu.SemaphoreType.DMA((GROUP,))] * 2
        + [pltpu.SemaphoreType.DMA((n_ctx,))] * 2
        + [pltpu.SemaphoreType.DMA((n_kvh,))] * 2,
        compiler_params=pltpu.CompilerParams(
            collective_id=0, has_side_effects=True, vmem_limit_bytes=60 << 20
        ),
        name="step",
    )(slot_request, slot_page, lengths, queries, keys, values, out_weight)


def solution(mesh):
    placed = (
        P(None, None, "kvh"),
        P("ctx", "kvh", None, None),
        P("ctx", "kvh", None, None),
        P("kvh", "ctx"),
        P(),
        P("ctx"),
        P("ctx"),
    )
    return jax.shard_map(
        functools.partial(per_device, mesh.shape["ctx"], mesh.shape["kvh"]),
        mesh=mesh, in_specs=placed, out_specs=P("kvh", "ctx"), check_vma=False,
    )
```

```python
import functools
import math

import jax
import jax.numpy as jnp
from jax import lax
from jax.experimental import pallas as pl
from jax.experimental.pallas import tpu as pltpu
from jax.sharding import PartitionSpec as P

QUERY_HEADS = 64
KEY_VALUE_HEADS = 8
DRAFT_TOKENS = 16
GROUP = QUERY_HEADS // KEY_VALUE_HEADS

MASKED = -1e30
FLOOR = -0.5e30
MESH = pl.DeviceIdType.MESH


def step(
    n_ctx, n_kvh, block,
    request_hbm, page_hbm, length_hbm, q_hbm, k_hbm, v_hbm, w_hbm, out_ref,
    request_ref, page_ref, length_ref, last_ref,
    q_in, q_rows, k_buf, v_buf, w_buf, ahead, top, mass, acc,
    o_out, stat_out, o_in, stat_in, att, share, share_in,
    small_sem, k_sem, v_sem, o_send, o_recv, t_send, t_recv, z_send, z_recv, x_send, x_recv, p_send, p_recv,
):
    c = lax.axis_index("ctx")
    k = lax.axis_index("kvh")
    slots, page_tokens, head_dim = k_buf.shape
    requests, rows = q_rows.shape[:2]
    per_owner, tokens = o_out.shape[1:3]
    heads = rows // tokens
    groups = n_ctx // heads
    blocks = slots // block
    scale2 = math.log2(math.e) / math.sqrt(head_dim)
    x, z = c // heads, lax.rem(c, heads)

    def fetch(source, target, sem):
        return pltpu.make_async_copy(source, target, sem)

    def k_copy(b):
        part = pl.ds(b * block, block)
        return fetch(k_hbm.at[part, 0], k_buf.at[part], k_sem.at[b])

    def v_copy(b):
        part = pl.ds(b * block, block)
        return fetch(v_hbm.at[part, 0], v_buf.at[part], v_sem.at[b])

    first = [
        fetch(request_hbm, request_ref, small_sem.at[0]),
        fetch(page_hbm, page_ref, small_sem.at[1]),
        fetch(length_hbm, length_ref, small_sem.at[2]),
        fetch(q_hbm, q_in, small_sem.at[3]),
    ]
    w_copy = fetch(w_hbm, w_buf, small_sem.at[4])
    for copy in first:
        copy.start()
    for b in range(blocks):
        k_copy(b).start()
        v_copy(b).start()
    w_copy.start()

    def ctx_device(j, i):
        return lax.rem(x + j, groups) * heads + lax.rem(z + i, heads)

    def kvh_device(i):
        return lax.rem(k + i, n_kvh)

    barrier = pltpu.get_barrier_semaphore()

    def greet_ctx(i, carry):
        pl.semaphore_signal(barrier, inc=1, device_id=(lax.rem(c + i, n_ctx), k), device_id_type=MESH)
        return carry

    def greet_kvh(i, carry):
        pl.semaphore_signal(barrier, inc=1, device_id=(c, kvh_device(i)), device_id_type=MESH)
        return carry

    lax.fori_loop(1, n_ctx, greet_ctx, 0)
    lax.fori_loop(1, n_kvh, greet_kvh, 0)

    top[slots] = jnp.full((1, rows), FLOOR, jnp.float32)
    mass[slots] = jnp.zeros((1, rows), jnp.float32)
    acc[slots] = jnp.zeros((head_dim, rows), jnp.float32)
    ahead[...] = lax.broadcasted_iota(jnp.int32, (page_tokens, rows), 0) - lax.rem(
        lax.broadcasted_iota(jnp.int32, (page_tokens, rows), 1), tokens
    )
    for copy in first:
        copy.wait()
    for r in range(requests):
        for h in range(heads):
            q_rows[r, h * tokens:(h + 1) * tokens, :] = q_in[r, :, h * head_dim:(h + 1) * head_dim]

    def visit(b, last):
        k_copy(b).wait()
        v_copy(b).wait()
        part = [b * block + u for u in range(block)]
        befores, scores, peaks, masses, outs = [], [], [], [], []
        for slot in part:
            r = request_ref[slot]
            known = jnp.minimum(r, requests - 1)
            limit = length_ref[known] - tokens - page_ref[slot] * page_tokens
            limit = jnp.where(r < requests, limit, -page_tokens)
            before = jnp.int32(slots)
            for n in range(requests):
                before = jnp.where(r == n, last[n], before)
            last = tuple(jnp.where(r == n, slot, last[n]) for n in range(requests))
            befores.append(before)
            s = lax.dot_general(
                k_buf[slot], q_rows[known], (((1,), (1,)), ((), ())), preferred_element_type=jnp.float32
            )
            s = jnp.where(ahead[...] <= limit, s, MASKED)
            scores.append(s)
            peaks.append(jnp.maximum(jnp.max(s, axis=0, keepdims=True), FLOOR))
        for slot, s, peak in zip(part, scores, peaks):
            weights = jnp.exp2((s - peak) * scale2)
            masses.append(jnp.sum(weights, axis=0, keepdims=True))
            outs.append(lax.dot_general(
                v_buf[slot], weights.astype(jnp.bfloat16), (((0,), (0,)), ((), ())),
                preferred_element_type=jnp.float32,
            ))
        for slot, before, peak, page_mass, page_out in zip(part, befores, peaks, masses, outs):
            old = top[before]
            new = jnp.maximum(old, peak)
            keep = jnp.exp2((old - new) * scale2)
            gain = jnp.exp2((peak - new) * scale2)
            top[slot] = new
            mass[slot] = mass[before] * keep + page_mass * gain
            acc[slot] = acc[before] * keep + page_out * gain
        return last

    last = lax.fori_loop(0, blocks, visit, (jnp.int32(slots),) * requests)
    for r in range(requests):
        last_ref[r] = last[r]

    def stat_copy(j, i):
        device, n = ctx_device(j, i), j * heads + i
        return pltpu.make_async_remote_copy(
            src_ref=stat_out.at[device], dst_ref=stat_in.at[c], send_sem=t_send.at[n], recv_sem=t_recv.at[n],
            device_id=(device, k), device_id_type=MESH,
        )

    def o_copy(j, i):
        device, n = ctx_device(j, i), j * heads + i
        return pltpu.make_async_remote_copy(
            src_ref=o_out.at[device], dst_ref=o_in.at[c], send_sem=o_send.at[n], recv_sem=o_recv.at[n],
            device_id=(device, k), device_id_type=MESH,
        )

    def z_copy(i):
        return pltpu.make_async_remote_copy(
            src_ref=att.at[c], dst_ref=att.at[c], send_sem=z_send.at[i], recv_sem=z_recv.at[i],
            device_id=(ctx_device(0, i), k), device_id_type=MESH,
        )

    def x_copy(j, i):
        source, n = x * heads + lax.rem(z + heads - i, heads), j * heads + i
        return pltpu.make_async_remote_copy(
            src_ref=att.at[source], dst_ref=att.at[source], send_sem=x_send.at[n], recv_sem=x_recv.at[n],
            device_id=(ctx_device(j, 0), k), device_id_type=MESH,
        )

    def share_copy(i):
        return pltpu.make_async_remote_copy(
            src_ref=share.at[kvh_device(i)], dst_ref=share_in.at[k], send_sem=p_send.at[i], recv_sem=p_recv.at[i],
            device_id=(c, kvh_device(i)), device_id_type=MESH,
        )

    pl.semaphore_wait(barrier, n_ctx + n_kvh - 2)

    lane = lax.broadcasted_iota(jnp.int32, (8, rows), 1)
    kind = lax.broadcasted_iota(jnp.int32, (8, rows), 0)

    def hand_out(n, carry):
        j = groups - 1 - n
        a = lax.rem(x + j, groups)
        packed = jnp.zeros((8, rows), jnp.float32)
        for i in range(per_owner):
            entry = last_ref[a * per_owner + i]
            packed = jnp.where(kind == i, top[entry], packed)
            packed = jnp.where(kind == per_owner + i, mass[entry], packed)
            turned = acc[entry].T.astype(jnp.bfloat16)
            for h in range(heads):
                o_out[a * heads + h, i] = turned[h * tokens:(h + 1) * tokens]
        slanted = pltpu.roll(packed, 0, 1, stride=tokens, stride_axis=0)
        for h in range(heads):
            moved = pltpu.roll(slanted, (rows - h * tokens) % rows, 1)
            moved = jnp.where(lane // tokens == kind, moved, 0.0)
            stat_out[a * heads + h] = jnp.sum(moved, axis=0, keepdims=True)

        def start(i, inner):
            stat_copy(j, i).start()
            o_copy(j, i).start()
            return inner

        lax.fori_loop(jnp.where(j == 0, 1, 0), heads, start, 0)
        return carry

    lax.fori_loop(0, groups, hand_out, 0)
    stat_in[c] = stat_out[c]
    o_in[c] = o_out[c]

    def each_ctx(act):
        def visit(n, carry):
            act(n // heads, lax.rem(n, heads))
            return carry

        lax.fori_loop(1, n_ctx, visit, 0)

    each_ctx(lambda j, i: stat_copy(j, i).wait_recv())
    stats = stat_in[...].reshape(n_ctx, head_dim)
    span = per_owner * tokens
    joined = jnp.max(stats, axis=0, keepdims=True)
    factor = jnp.exp2((stats - joined) * scale2)
    masses = pltpu.roll(stats, head_dim - span, 1)
    column = lax.broadcasted_iota(jnp.int32, stats.shape, 1)
    factor = jnp.where(column < span, factor, 0.0)
    total = jnp.sum(factor * masses, axis=0, keepdims=True)
    total = jnp.where(column[:1] < span, total, 1.0)
    factor = (factor / total).T
    each_ctx(lambda j, i: o_copy(j, i).wait_recv())
    attended = jnp.zeros((span, head_dim), jnp.float32)
    for s in range(n_ctx):
        attended += factor[:span, s:s + 1] * o_in[s].reshape(span, head_dim).astype(jnp.float32)
    att[c] = attended.astype(jnp.bfloat16).reshape(per_owner, tokens, head_dim)

    near_first = [i for pair in zip(range(1, heads // 2), range(heads - 1, heads // 2, -1)) for i in pair] + [heads // 2]
    beside = [1, groups - 1] + list(range(2, groups - 1))
    for i in near_first:
        z_copy(i).start()
    for j in beside:
        x_copy(j, 0).start()
    for i in near_first:
        z_copy(i).wait_recv()
        for j in beside:
            x_copy(j, i).start()
    w_copy.wait()
    part = share.shape[1]
    per_group = span // part

    def project(j):
        a = lax.rem(x + groups - j, groups)
        operand = jnp.concatenate([att[a * heads + h].reshape(span, head_dim) for h in range(heads)], axis=1)
        product = jnp.dot(operand, w_buf[...], preferred_element_type=jnp.float32).astype(jnp.bfloat16)
        for d in range(per_group):
            share[a * per_group + d] = product[d * part:(d + 1) * part]
        for d in range(per_group):
            target = a * per_group + d

            @pl.when(target != k)
            def _(target=target):
                share_copy(lax.rem(target + n_kvh - k, n_kvh)).start()

    project(0)
    for j in beside:
        for i in [0] + near_first:
            x_copy(j, i).wait_recv()
        project(j)

    def finish_share(i, carry):
        share_copy(i).wait()
        return carry

    share_in[k] = share[k]

    def settle(j, i):
        stat_copy(j, i).wait_send()
        o_copy(j, i).wait_send()

    each_ctx(settle)
    for i in near_first:
        z_copy(i).wait_send()
    for i in [0] + near_first:
        for j in beside:
            x_copy(j, i).wait_send()
    lax.fori_loop(1, n_kvh, finish_share, 0)
    summed = share_in[0].astype(jnp.float32)
    for d in range(1, n_kvh):
        summed += share_in[d].astype(jnp.float32)
    out_ref[...] = summed.astype(jnp.bfloat16)


def per_device(n_ctx, n_kvh, queries, keys, values, out_weight, lengths, slot_request, slot_page):
    requests = queries.shape[0]
    slots, _, page_tokens, head_dim = keys.shape
    rows = DRAFT_TOKENS * GROUP
    per_owner = requests * GROUP // n_ctx
    owned = (n_ctx, per_owner, DRAFT_TOKENS, head_dim)
    total_rows = requests * DRAFT_TOKENS
    columns = out_weight.shape[1]
    block = 32
    blocks = slots // block
    shared = (n_kvh, total_rows // n_kvh, columns)
    return pl.pallas_call(
        functools.partial(step, n_ctx, n_kvh, block),
        out_shape=jax.ShapeDtypeStruct(shared[1:], jnp.bfloat16),
        in_specs=[pl.BlockSpec(memory_space=pltpu.HBM)] * 7,
        out_specs=pl.BlockSpec(memory_space=pltpu.VMEM),
        scratch_shapes=[
            pltpu.SMEM((slots,), jnp.int32),
            pltpu.SMEM((slots,), jnp.int32),
            pltpu.SMEM((requests,), jnp.int32),
            pltpu.SMEM((requests,), jnp.int32),
            pltpu.VMEM(queries.shape, jnp.bfloat16),
            pltpu.VMEM((requests, rows, head_dim), jnp.bfloat16),
            pltpu.VMEM((slots, page_tokens, head_dim), jnp.bfloat16),
            pltpu.VMEM((slots, page_tokens, head_dim), jnp.bfloat16),
            pltpu.VMEM(out_weight.shape, jnp.bfloat16),
            pltpu.VMEM((page_tokens, rows), jnp.int32),
            pltpu.VMEM((slots + 1, 1, rows), jnp.float32),
            pltpu.VMEM((slots + 1, 1, rows), jnp.float32),
            pltpu.VMEM((slots + 1, head_dim, rows), jnp.float32),
            pltpu.VMEM(owned, jnp.bfloat16),
            pltpu.VMEM((n_ctx, 1, head_dim), jnp.float32),
            pltpu.VMEM(owned, jnp.bfloat16),
            pltpu.VMEM((n_ctx, 1, head_dim), jnp.float32),
            pltpu.VMEM(owned, jnp.bfloat16),
            pltpu.VMEM(shared, jnp.bfloat16),
            pltpu.VMEM(shared, jnp.bfloat16),
            pltpu.SemaphoreType.DMA((5,)),
            pltpu.SemaphoreType.DMA((blocks,)),
            pltpu.SemaphoreType.DMA((blocks,)),
        ]
        + [pltpu.SemaphoreType.DMA((n_ctx,))] * 4
        + [pltpu.SemaphoreType.DMA((GROUP,))] * 2
        + [pltpu.SemaphoreType.DMA((n_ctx,))] * 2
        + [pltpu.SemaphoreType.DMA((n_kvh,))] * 2,
        compiler_params=pltpu.CompilerParams(
            collective_id=0, has_side_effects=True, vmem_limit_bytes=60 << 20
        ),
        name="step",
    )(slot_request, slot_page, lengths, queries, keys, values, out_weight)


def solution(mesh):
    placed = (
        P(None, None, "kvh"),
        P("ctx", "kvh", None, None),
        P("ctx", "kvh", None, None),
        P("kvh", "ctx"),
        P(),
        P("ctx"),
        P("ctx"),
    )
    return jax.shard_map(
        functools.partial(per_device, mesh.shape["ctx"], mesh.shape["kvh"]),
        mesh=mesh, in_specs=placed, out_specs=P("kvh", "ctx"), check_vma=False,
    )
```

```python
import functools
import math

import jax
import jax.numpy as jnp
from jax import lax
from jax.experimental import pallas as pl
from jax.experimental.pallas import tpu as pltpu
from jax.sharding import PartitionSpec as P

QUERY_HEADS = 64
KEY_VALUE_HEADS = 8
DRAFT_TOKENS = 16
GROUP = QUERY_HEADS // KEY_VALUE_HEADS

MASKED = -1e30
FLOOR = -0.5e30
MESH = pl.DeviceIdType.MESH


def step(
    n_ctx, n_kvh, block,
    request_hbm, page_hbm, length_hbm, q_hbm, k_hbm, v_hbm, w_hbm, out_ref,
    request_ref, page_ref, length_ref, last_ref,
    q_in, q_rows, k_buf, v_buf, w_buf, ahead, top, mass, acc,
    o_out, stat_out, o_in, stat_in, att, share, share_in,
    small_sem, k_sem, v_sem, o_send, o_recv, t_send, t_recv, z_send, z_recv, x_send, x_recv, p_send, p_recv,
):
    c = lax.axis_index("ctx")
    k = lax.axis_index("kvh")
    slots, page_tokens, head_dim = k_buf.shape
    requests, rows = q_rows.shape[:2]
    per_owner, tokens = o_out.shape[1:3]
    heads = rows // tokens
    groups = n_ctx // heads
    blocks = slots // block
    scale2 = math.log2(math.e) / math.sqrt(head_dim)
    x, z = c // heads, lax.rem(c, heads)

    def fetch(source, target, sem):
        return pltpu.make_async_copy(source, target, sem)

    def k_copy(b):
        part = pl.ds(b * block, block)
        return fetch(k_hbm.at[part, 0], k_buf.at[part], k_sem.at[b])

    def v_copy(b):
        part = pl.ds(b * block, block)
        return fetch(v_hbm.at[part, 0], v_buf.at[part], v_sem.at[b])

    first = [
        fetch(request_hbm, request_ref, small_sem.at[0]),
        fetch(page_hbm, page_ref, small_sem.at[1]),
        fetch(length_hbm, length_ref, small_sem.at[2]),
        fetch(q_hbm, q_in, small_sem.at[3]),
    ]
    w_copy = fetch(w_hbm, w_buf, small_sem.at[4])
    for copy in first:
        copy.start()
    for b in range(blocks):
        k_copy(b).start()
        v_copy(b).start()
    w_copy.start()

    def ctx_device(j, i):
        return lax.rem(x + j, groups) * heads + lax.rem(z + i, heads)

    def kvh_device(i):
        return lax.rem(k + i, n_kvh)

    barrier = pltpu.get_barrier_semaphore()

    def greet_ctx(i, carry):
        pl.semaphore_signal(barrier, inc=1, device_id=(lax.rem(c + i, n_ctx), k), device_id_type=MESH)
        return carry

    def greet_kvh(i, carry):
        pl.semaphore_signal(barrier, inc=1, device_id=(c, kvh_device(i)), device_id_type=MESH)
        return carry

    lax.fori_loop(1, n_ctx, greet_ctx, 0)
    lax.fori_loop(1, n_kvh, greet_kvh, 0)

    top[slots] = jnp.full((1, rows), FLOOR, jnp.float32)
    mass[slots] = jnp.zeros((1, rows), jnp.float32)
    acc[slots] = jnp.zeros((head_dim, rows), jnp.float32)
    ahead[...] = lax.broadcasted_iota(jnp.int32, (page_tokens, rows), 0) - lax.rem(
        lax.broadcasted_iota(jnp.int32, (page_tokens, rows), 1), tokens
    )
    for copy in first:
        copy.wait()
    for r in range(requests):
        for h in range(heads):
            q_rows[r, h * tokens:(h + 1) * tokens, :] = q_in[r, :, h * head_dim:(h + 1) * head_dim]

    def visit(b, last):
        k_copy(b).wait()
        part = [b * block + u for u in range(block)]
        befores, scores, peaks, masses, outs = [], [], [], [], []
        for slot in part:
            r = request_ref[slot]
            known = jnp.minimum(r, requests - 1)
            limit = length_ref[known] - tokens - page_ref[slot] * page_tokens
            limit = jnp.where(r < requests, limit, -page_tokens)
            before = jnp.int32(slots)
            for n in range(requests):
                before = jnp.where(r == n, last[n], before)
            last = tuple(jnp.where(r == n, slot, last[n]) for n in range(requests))
            befores.append(before)
            s = lax.dot_general(
                k_buf[slot], q_rows[known], (((1,), (1,)), ((), ())), preferred_element_type=jnp.float32
            )
            s = jnp.where(ahead[...] <= limit, s, MASKED)
            scores.append(s)
            peaks.append(jnp.maximum(jnp.max(s, axis=0, keepdims=True), FLOOR))
        v_copy(b).wait()
        for slot, s, peak in zip(part, scores, peaks):
            weights = jnp.exp2((s - peak) * scale2)
            masses.append(jnp.sum(weights, axis=0, keepdims=True))
            outs.append(lax.dot_general(
                v_buf[slot], weights.astype(jnp.bfloat16), (((0,), (0,)), ((), ())),
                preferred_element_type=jnp.float32,
            ))
        for slot, before, peak, page_mass, page_out in zip(part, befores, peaks, masses, outs):
            old = top[before]
            new = jnp.maximum(old, peak)
            keep = jnp.exp2((old - new) * scale2)
            gain = jnp.exp2((peak - new) * scale2)
            top[slot] = new
            mass[slot] = mass[before] * keep + page_mass * gain
            acc[slot] = acc[before] * keep + page_out * gain
        return last

    last = lax.fori_loop(0, blocks, visit, (jnp.int32(slots),) * requests)
    for r in range(requests):
        last_ref[r] = last[r]

    def stat_copy(j, i):
        device, n = ctx_device(j, i), j * heads + i
        return pltpu.make_async_remote_copy(
            src_ref=stat_out.at[device], dst_ref=stat_in.at[c], send_sem=t_send.at[n], recv_sem=t_recv.at[n],
            device_id=(device, k), device_id_type=MESH,
        )

    def o_copy(j, i):
        device, n = ctx_device(j, i), j * heads + i
        return pltpu.make_async_remote_copy(
            src_ref=o_out.at[device], dst_ref=o_in.at[c], send_sem=o_send.at[n], recv_sem=o_recv.at[n],
            device_id=(device, k), device_id_type=MESH,
        )

    def z_copy(i):
        return pltpu.make_async_remote_copy(
            src_ref=att.at[c], dst_ref=att.at[c], send_sem=z_send.at[i], recv_sem=z_recv.at[i],
            device_id=(ctx_device(0, i), k), device_id_type=MESH,
        )

    def x_copy(j, i):
        source, n = x * heads + lax.rem(z + heads - i, heads), j * heads + i
        return pltpu.make_async_remote_copy(
            src_ref=att.at[source], dst_ref=att.at[source], send_sem=x_send.at[n], recv_sem=x_recv.at[n],
            device_id=(ctx_device(j, 0), k), device_id_type=MESH,
        )

    def share_copy(i):
        return pltpu.make_async_remote_copy(
            src_ref=share.at[kvh_device(i)], dst_ref=share_in.at[k], send_sem=p_send.at[i], recv_sem=p_recv.at[i],
            device_id=(c, kvh_device(i)), device_id_type=MESH,
        )

    pl.semaphore_wait(barrier, n_ctx + n_kvh - 2)

    lane = lax.broadcasted_iota(jnp.int32, (8, rows), 1)
    kind = lax.broadcasted_iota(jnp.int32, (8, rows), 0)

    def hand_out(n, carry):
        j = groups - 1 - n
        a = lax.rem(x + j, groups)
        packed = jnp.zeros((8, rows), jnp.float32)
        for i in range(per_owner):
            entry = last_ref[a * per_owner + i]
            packed = jnp.where(kind == i, top[entry], packed)
            packed = jnp.where(kind == per_owner + i, mass[entry], packed)
            turned = acc[entry].T.astype(jnp.bfloat16)
            for h in range(heads):
                o_out[a * heads + h, i] = turned[h * tokens:(h + 1) * tokens]
        slanted = pltpu.roll(packed, 0, 1, stride=tokens, stride_axis=0)
        for h in range(heads):
            moved = pltpu.roll(slanted, (rows - h * tokens) % rows, 1)
            moved = jnp.where(lane // tokens == kind, moved, 0.0)
            stat_out[a * heads + h] = jnp.sum(moved, axis=0, keepdims=True)

        def start(i, inner):
            stat_copy(j, i).start()
            o_copy(j, i).start()
            return inner

        lax.fori_loop(jnp.where(j == 0, 1, 0), heads, start, 0)
        return carry

    lax.fori_loop(0, groups, hand_out, 0)
    stat_in[c] = stat_out[c]
    o_in[c] = o_out[c]

    def each_ctx(act):
        def visit(n, carry):
            act(n // heads, lax.rem(n, heads))
            return carry

        lax.fori_loop(1, n_ctx, visit, 0)

    each_ctx(lambda j, i: stat_copy(j, i).wait_recv())
    stats = stat_in[...].reshape(n_ctx, head_dim)
    span = per_owner * tokens
    joined = jnp.max(stats, axis=0, keepdims=True)
    factor = jnp.exp2((stats - joined) * scale2)
    masses = pltpu.roll(stats, head_dim - span, 1)
    column = lax.broadcasted_iota(jnp.int32, stats.shape, 1)
    factor = jnp.where(column < span, factor, 0.0)
    total = jnp.sum(factor * masses, axis=0, keepdims=True)
    total = jnp.where(column[:1] < span, total, 1.0)
    factor = (factor / total).T
    each_ctx(lambda j, i: o_copy(j, i).wait_recv())
    attended = jnp.zeros((span, head_dim), jnp.float32)
    for s in range(n_ctx):
        attended += factor[:span, s:s + 1] * o_in[s].reshape(span, head_dim).astype(jnp.float32)
    att[c] = attended.astype(jnp.bfloat16).reshape(per_owner, tokens, head_dim)

    near_first = [i for pair in zip(range(1, heads // 2), range(heads - 1, heads // 2, -1)) for i in pair] + [heads // 2]
    beside = [1, groups - 1] + list(range(2, groups - 1))
    for i in near_first:
        z_copy(i).start()
    for j in beside:
        x_copy(j, 0).start()
    for i in near_first:
        z_copy(i).wait_recv()
        for j in beside:
            x_copy(j, i).start()
    w_copy.wait()
    part = share.shape[1]
    per_group = span // part

    def project(j):
        a = lax.rem(x + groups - j, groups)
        operand = jnp.concatenate([att[a * heads + h].reshape(span, head_dim) for h in range(heads)], axis=1)
        product = jnp.dot(operand, w_buf[...], preferred_element_type=jnp.float32).astype(jnp.bfloat16)
        for d in range(per_group):
            share[a * per_group + d] = product[d * part:(d + 1) * part]
        for d in range(per_group):
            target = a * per_group + d

            @pl.when(target != k)
            def _(target=target):
                share_copy(lax.rem(target + n_kvh - k, n_kvh)).start()

    project(0)
    for j in beside:
        for i in [0] + near_first:
            x_copy(j, i).wait_recv()
        project(j)

    def finish_share(i, carry):
        share_copy(i).wait()
        return carry

    share_in[k] = share[k]

    def settle(j, i):
        stat_copy(j, i).wait_send()
        o_copy(j, i).wait_send()

    each_ctx(settle)
    for i in near_first:
        z_copy(i).wait_send()
    for i in [0] + near_first:
        for j in beside:
            x_copy(j, i).wait_send()
    lax.fori_loop(1, n_kvh, finish_share, 0)
    summed = share_in[0].astype(jnp.float32)
    for d in range(1, n_kvh):
        summed += share_in[d].astype(jnp.float32)
    out_ref[...] = summed.astype(jnp.bfloat16)


def per_device(n_ctx, n_kvh, queries, keys, values, out_weight, lengths, slot_request, slot_page):
    requests = queries.shape[0]
    slots, _, page_tokens, head_dim = keys.shape
    rows = DRAFT_TOKENS * GROUP
    per_owner = requests * GROUP // n_ctx
    owned = (n_ctx, per_owner, DRAFT_TOKENS, head_dim)
    total_rows = requests * DRAFT_TOKENS
    columns = out_weight.shape[1]
    block = 32
    blocks = slots // block
    shared = (n_kvh, total_rows // n_kvh, columns)
    return pl.pallas_call(
        functools.partial(step, n_ctx, n_kvh, block),
        out_shape=jax.ShapeDtypeStruct(shared[1:], jnp.bfloat16),
        in_specs=[pl.BlockSpec(memory_space=pltpu.HBM)] * 7,
        out_specs=pl.BlockSpec(memory_space=pltpu.VMEM),
        scratch_shapes=[
            pltpu.SMEM((slots,), jnp.int32),
            pltpu.SMEM((slots,), jnp.int32),
            pltpu.SMEM((requests,), jnp.int32),
            pltpu.SMEM((requests,), jnp.int32),
            pltpu.VMEM(queries.shape, jnp.bfloat16),
            pltpu.VMEM((requests, rows, head_dim), jnp.bfloat16),
            pltpu.VMEM((slots, page_tokens, head_dim), jnp.bfloat16),
            pltpu.VMEM((slots, page_tokens, head_dim), jnp.bfloat16),
            pltpu.VMEM(out_weight.shape, jnp.bfloat16),
            pltpu.VMEM((page_tokens, rows), jnp.int32),
            pltpu.VMEM((slots + 1, 1, rows), jnp.float32),
            pltpu.VMEM((slots + 1, 1, rows), jnp.float32),
            pltpu.VMEM((slots + 1, head_dim, rows), jnp.float32),
            pltpu.VMEM(owned, jnp.bfloat16),
            pltpu.VMEM((n_ctx, 1, head_dim), jnp.float32),
            pltpu.VMEM(owned, jnp.bfloat16),
            pltpu.VMEM((n_ctx, 1, head_dim), jnp.float32),
            pltpu.VMEM(owned, jnp.bfloat16),
            pltpu.VMEM(shared, jnp.bfloat16),
            pltpu.VMEM(shared, jnp.bfloat16),
            pltpu.SemaphoreType.DMA((5,)),
            pltpu.SemaphoreType.DMA((blocks,)),
            pltpu.SemaphoreType.DMA((blocks,)),
        ]
        + [pltpu.SemaphoreType.DMA((n_ctx,))] * 4
        + [pltpu.SemaphoreType.DMA((GROUP,))] * 2
        + [pltpu.SemaphoreType.DMA((n_ctx,))] * 2
        + [pltpu.SemaphoreType.DMA((n_kvh,))] * 2,
        compiler_params=pltpu.CompilerParams(
            collective_id=0, has_side_effects=True, vmem_limit_bytes=60 << 20
        ),
        name="step",
    )(slot_request, slot_page, lengths, queries, keys, values, out_weight)


def solution(mesh):
    placed = (
        P(None, None, "kvh"),
        P("ctx", "kvh", None, None),
        P("ctx", "kvh", None, None),
        P("kvh", "ctx"),
        P(),
        P("ctx"),
        P("ctx"),
    )
    return jax.shard_map(
        functools.partial(per_device, mesh.shape["ctx"], mesh.shape["kvh"]),
        mesh=mesh, in_specs=placed, out_specs=P("kvh", "ctx"), check_vma=False,
    )
```

```python
import functools
import math

import jax
import jax.numpy as jnp
from jax import lax
from jax.experimental import pallas as pl
from jax.experimental.pallas import tpu as pltpu
from jax.sharding import PartitionSpec as P

QUERY_HEADS = 64
KEY_VALUE_HEADS = 8
DRAFT_TOKENS = 16
GROUP = QUERY_HEADS // KEY_VALUE_HEADS

MASKED = -1e30
FLOOR = -0.5e30
MESH = pl.DeviceIdType.MESH


def step(
    n_ctx, n_kvh, block,
    request_hbm, page_hbm, length_hbm, q_hbm, k_hbm, v_hbm, w_hbm, out_ref,
    request_ref, page_ref, length_ref, last_ref,
    q_in, q_rows, k_buf, v_buf, w_buf, ahead, top, mass, acc,
    o_out, stat_out, o_in, stat_in, att, share, share_in,
    small_sem, k_sem, v_sem, o_send, o_recv, t_send, t_recv, z_send, z_recv, x_send, x_recv, p_send, p_recv,
):
    c = lax.axis_index("ctx")
    k = lax.axis_index("kvh")
    slots, page_tokens, head_dim = k_buf.shape
    requests, rows = q_rows.shape[:2]
    per_owner, tokens = o_out.shape[1:3]
    heads = rows // tokens
    groups = n_ctx // heads
    sizes = [16, 48]
    starts = [sum(sizes[:b]) for b in range(len(sizes))]
    blocks = len(sizes)
    scale2 = math.log2(math.e) / math.sqrt(head_dim)
    x, z = c // heads, lax.rem(c, heads)

    def fetch(source, target, sem):
        return pltpu.make_async_copy(source, target, sem)

    def k_copy(b):
        part = pl.ds(starts[b], sizes[b])
        return fetch(k_hbm.at[part, 0], k_buf.at[part], k_sem.at[b])

    def v_copy(b):
        part = pl.ds(starts[b], sizes[b])
        return fetch(v_hbm.at[part, 0], v_buf.at[part], v_sem.at[b])

    first = [
        fetch(request_hbm, request_ref, small_sem.at[0]),
        fetch(page_hbm, page_ref, small_sem.at[1]),
        fetch(length_hbm, length_ref, small_sem.at[2]),
        fetch(q_hbm, q_in, small_sem.at[3]),
    ]
    w_copy = fetch(w_hbm, w_buf, small_sem.at[4])
    for copy in first:
        copy.start()
    for b in range(blocks):
        k_copy(b).start()
        v_copy(b).start()
    w_copy.start()

    def ctx_device(j, i):
        return lax.rem(x + j, groups) * heads + lax.rem(z + i, heads)

    def kvh_device(i):
        return lax.rem(k + i, n_kvh)

    barrier = pltpu.get_barrier_semaphore()

    def greet_ctx(i, carry):
        pl.semaphore_signal(barrier, inc=1, device_id=(lax.rem(c + i, n_ctx), k), device_id_type=MESH)
        return carry

    def greet_kvh(i, carry):
        pl.semaphore_signal(barrier, inc=1, device_id=(c, kvh_device(i)), device_id_type=MESH)
        return carry

    lax.fori_loop(1, n_ctx, greet_ctx, 0)
    lax.fori_loop(1, n_kvh, greet_kvh, 0)

    top[slots] = jnp.full((1, rows), FLOOR, jnp.float32)
    mass[slots] = jnp.zeros((1, rows), jnp.float32)
    acc[slots] = jnp.zeros((head_dim, rows), jnp.float32)
    ahead[...] = lax.broadcasted_iota(jnp.int32, (page_tokens, rows), 0) - lax.rem(
        lax.broadcasted_iota(jnp.int32, (page_tokens, rows), 1), tokens
    )
    for copy in first:
        copy.wait()
    for r in range(requests):
        for h in range(heads):
            q_rows[r, h * tokens:(h + 1) * tokens, :] = q_in[r, :, h * head_dim:(h + 1) * head_dim]

    def visit(b, last):
        k_copy(b).wait()
        part = [starts[b] + u for u in range(sizes[b])]
        befores, scores, peaks, masses, outs = [], [], [], [], []
        for slot in part:
            r = request_ref[slot]
            known = jnp.minimum(r, requests - 1)
            limit = length_ref[known] - tokens - page_ref[slot] * page_tokens
            limit = jnp.where(r < requests, limit, -page_tokens)
            before = jnp.int32(slots)
            for n in range(requests):
                before = jnp.where(r == n, last[n], before)
            last = tuple(jnp.where(r == n, slot, last[n]) for n in range(requests))
            befores.append(before)
            s = lax.dot_general(
                k_buf[slot], q_rows[known], (((1,), (1,)), ((), ())), preferred_element_type=jnp.float32
            )
            s = jnp.where(ahead[...] <= limit, s, MASKED)
            scores.append(s)
            peaks.append(jnp.maximum(jnp.max(s, axis=0, keepdims=True), FLOOR))
        v_copy(b).wait()
        for slot, s, peak in zip(part, scores, peaks):
            weights = jnp.exp2((s - peak) * scale2)
            masses.append(jnp.sum(weights, axis=0, keepdims=True))
            outs.append(lax.dot_general(
                v_buf[slot], weights.astype(jnp.bfloat16), (((0,), (0,)), ((), ())),
                preferred_element_type=jnp.float32,
            ))
        for slot, before, peak, page_mass, page_out in zip(part, befores, peaks, masses, outs):
            old = top[before]
            new = jnp.maximum(old, peak)
            keep = jnp.exp2((old - new) * scale2)
            gain = jnp.exp2((peak - new) * scale2)
            top[slot] = new
            mass[slot] = mass[before] * keep + page_mass * gain
            acc[slot] = acc[before] * keep + page_out * gain
        return last

    last = (jnp.int32(slots),) * requests
    for b in range(blocks):
        last = visit(b, last)
    for r in range(requests):
        last_ref[r] = last[r]

    def stat_copy(j, i):
        device, n = ctx_device(j, i), j * heads + i
        return pltpu.make_async_remote_copy(
            src_ref=stat_out.at[device], dst_ref=stat_in.at[c], send_sem=t_send.at[n], recv_sem=t_recv.at[n],
            device_id=(device, k), device_id_type=MESH,
        )

    def o_copy(j, i):
        device, n = ctx_device(j, i), j * heads + i
        return pltpu.make_async_remote_copy(
            src_ref=o_out.at[device], dst_ref=o_in.at[c], send_sem=o_send.at[n], recv_sem=o_recv.at[n],
            device_id=(device, k), device_id_type=MESH,
        )

    def z_copy(i):
        return pltpu.make_async_remote_copy(
            src_ref=att.at[c], dst_ref=att.at[c], send_sem=z_send.at[i], recv_sem=z_recv.at[i],
            device_id=(ctx_device(0, i), k), device_id_type=MESH,
        )

    def x_copy(j, i):
        source, n = x * heads + lax.rem(z + heads - i, heads), j * heads + i
        return pltpu.make_async_remote_copy(
            src_ref=att.at[source], dst_ref=att.at[source], send_sem=x_send.at[n], recv_sem=x_recv.at[n],
            device_id=(ctx_device(j, 0), k), device_id_type=MESH,
        )

    def share_copy(i):
        return pltpu.make_async_remote_copy(
            src_ref=share.at[kvh_device(i)], dst_ref=share_in.at[k], send_sem=p_send.at[i], recv_sem=p_recv.at[i],
            device_id=(c, kvh_device(i)), device_id_type=MESH,
        )

    pl.semaphore_wait(barrier, n_ctx + n_kvh - 2)

    lane = lax.broadcasted_iota(jnp.int32, (8, rows), 1)
    kind = lax.broadcasted_iota(jnp.int32, (8, rows), 0)

    def hand_out(n, carry):
        j = groups - 1 - n
        a = lax.rem(x + j, groups)
        packed = jnp.zeros((8, rows), jnp.float32)
        for i in range(per_owner):
            entry = last_ref[a * per_owner + i]
            packed = jnp.where(kind == i, top[entry], packed)
            packed = jnp.where(kind == per_owner + i, mass[entry], packed)
            turned = acc[entry].T.astype(jnp.bfloat16)
            for h in range(heads):
                o_out[a * heads + h, i] = turned[h * tokens:(h + 1) * tokens]
        slanted = pltpu.roll(packed, 0, 1, stride=tokens, stride_axis=0)
        for h in range(heads):
            moved = pltpu.roll(slanted, (rows - h * tokens) % rows, 1)
            moved = jnp.where(lane // tokens == kind, moved, 0.0)
            stat_out[a * heads + h] = jnp.sum(moved, axis=0, keepdims=True)

        def start(i, inner):
            stat_copy(j, i).start()
            o_copy(j, i).start()
            return inner

        lax.fori_loop(jnp.where(j == 0, 1, 0), heads, start, 0)
        return carry

    lax.fori_loop(0, groups, hand_out, 0)
    stat_in[c] = stat_out[c]
    o_in[c] = o_out[c]

    def each_ctx(act):
        def visit(n, carry):
            act(n // heads, lax.rem(n, heads))
            return carry

        lax.fori_loop(1, n_ctx, visit, 0)

    each_ctx(lambda j, i: stat_copy(j, i).wait_recv())
    stats = stat_in[...].reshape(n_ctx, head_dim)
    span = per_owner * tokens
    joined = jnp.max(stats, axis=0, keepdims=True)
    factor = jnp.exp2((stats - joined) * scale2)
    masses = pltpu.roll(stats, head_dim - span, 1)
    column = lax.broadcasted_iota(jnp.int32, stats.shape, 1)
    factor = jnp.where(column < span, factor, 0.0)
    total = jnp.sum(factor * masses, axis=0, keepdims=True)
    total = jnp.where(column[:1] < span, total, 1.0)
    factor = (factor / total).T
    each_ctx(lambda j, i: o_copy(j, i).wait_recv())
    attended = jnp.zeros((span, head_dim), jnp.float32)
    for s in range(n_ctx):
        attended += factor[:span, s:s + 1] * o_in[s].reshape(span, head_dim).astype(jnp.float32)
    att[c] = attended.astype(jnp.bfloat16).reshape(per_owner, tokens, head_dim)

    near_first = [i for pair in zip(range(1, heads // 2), range(heads - 1, heads // 2, -1)) for i in pair] + [heads // 2]
    beside = [1, groups - 1] + list(range(2, groups - 1))
    for i in near_first:
        z_copy(i).start()
    for j in reversed(beside):
        x_copy(j, 0).start()
    for i in near_first:
        z_copy(i).wait_recv()
        for j in reversed(beside):
            x_copy(j, i).start()
    w_copy.wait()
    part = share.shape[1]
    per_group = span // part

    def project(j):
        a = lax.rem(x + groups - j, groups)
        operand = jnp.concatenate([att[a * heads + h].reshape(span, head_dim) for h in range(heads)], axis=1)
        product = jnp.dot(operand, w_buf[...], preferred_element_type=jnp.float32).astype(jnp.bfloat16)
        for d in range(per_group):
            share[a * per_group + d] = product[d * part:(d + 1) * part]
        for d in range(per_group):
            target = a * per_group + d

            @pl.when(target != k)
            def _(target=target):
                share_copy(lax.rem(target + n_kvh - k, n_kvh)).start()

    project(0)
    for j in beside:
        for i in [0] + near_first:
            x_copy(j, i).wait_recv()
        project(j)

    def finish_share(i, carry):
        share_copy(i).wait()
        return carry

    share_in[k] = share[k]

    def settle(j, i):
        stat_copy(j, i).wait_send()
        o_copy(j, i).wait_send()

    each_ctx(settle)
    for i in near_first:
        z_copy(i).wait_send()
    for i in [0] + near_first:
        for j in beside:
            x_copy(j, i).wait_send()
    lax.fori_loop(1, n_kvh, finish_share, 0)
    summed = share_in[0].astype(jnp.float32)
    for d in range(1, n_kvh):
        summed += share_in[d].astype(jnp.float32)
    out_ref[...] = summed.astype(jnp.bfloat16)


def per_device(n_ctx, n_kvh, queries, keys, values, out_weight, lengths, slot_request, slot_page):
    requests = queries.shape[0]
    slots, _, page_tokens, head_dim = keys.shape
    rows = DRAFT_TOKENS * GROUP
    per_owner = requests * GROUP // n_ctx
    owned = (n_ctx, per_owner, DRAFT_TOKENS, head_dim)
    total_rows = requests * DRAFT_TOKENS
    columns = out_weight.shape[1]
    block = 32
    blocks = 4
    shared = (n_kvh, total_rows // n_kvh, columns)
    return pl.pallas_call(
        functools.partial(step, n_ctx, n_kvh, block),
        out_shape=jax.ShapeDtypeStruct(shared[1:], jnp.bfloat16),
        in_specs=[pl.BlockSpec(memory_space=pltpu.HBM)] * 7,
        out_specs=pl.BlockSpec(memory_space=pltpu.VMEM),
        scratch_shapes=[
            pltpu.SMEM((slots,), jnp.int32),
            pltpu.SMEM((slots,), jnp.int32),
            pltpu.SMEM((requests,), jnp.int32),
            pltpu.SMEM((requests,), jnp.int32),
            pltpu.VMEM(queries.shape, jnp.bfloat16),
            pltpu.VMEM((requests, rows, head_dim), jnp.bfloat16),
            pltpu.VMEM((slots, page_tokens, head_dim), jnp.bfloat16),
            pltpu.VMEM((slots, page_tokens, head_dim), jnp.bfloat16),
            pltpu.VMEM(out_weight.shape, jnp.bfloat16),
            pltpu.VMEM((page_tokens, rows), jnp.int32),
            pltpu.VMEM((slots + 1, 1, rows), jnp.float32),
            pltpu.VMEM((slots + 1, 1, rows), jnp.float32),
            pltpu.VMEM((slots + 1, head_dim, rows), jnp.float32),
            pltpu.VMEM(owned, jnp.bfloat16),
            pltpu.VMEM((n_ctx, 1, head_dim), jnp.float32),
            pltpu.VMEM(owned, jnp.bfloat16),
            pltpu.VMEM((n_ctx, 1, head_dim), jnp.float32),
            pltpu.VMEM(owned, jnp.bfloat16),
            pltpu.VMEM(shared, jnp.bfloat16),
            pltpu.VMEM(shared, jnp.bfloat16),
            pltpu.SemaphoreType.DMA((5,)),
            pltpu.SemaphoreType.DMA((blocks,)),
            pltpu.SemaphoreType.DMA((blocks,)),
        ]
        + [pltpu.SemaphoreType.DMA((n_ctx,))] * 4
        + [pltpu.SemaphoreType.DMA((GROUP,))] * 2
        + [pltpu.SemaphoreType.DMA((n_ctx,))] * 2
        + [pltpu.SemaphoreType.DMA((n_kvh,))] * 2,
        compiler_params=pltpu.CompilerParams(
            collective_id=0, has_side_effects=True, vmem_limit_bytes=60 << 20
        ),
        name="step",
    )(slot_request, slot_page, lengths, queries, keys, values, out_weight)


def solution(mesh):
    placed = (
        P(None, None, "kvh"),
        P("ctx", "kvh", None, None),
        P("ctx", "kvh", None, None),
        P("kvh", "ctx"),
        P(),
        P("ctx"),
        P("ctx"),
    )
    return jax.shard_map(
        functools.partial(per_device, mesh.shape["ctx"], mesh.shape["kvh"]),
        mesh=mesh, in_specs=placed, out_specs=P("kvh", "ctx"), check_vma=False,
    )
```
